512 devices in a mesh: cont: 16 (over x, y), net: 32 (over z, core).
Axes of the slice: x: 4, y: 4, z: 16, core: 2. Of those that a mesh axis runs over, the one named last changes fastest.
Arguments:
- angles: float32 [1024, 16384], P('cont', 'net'), may hold values from -6 to 6
- lam_from: float32 [1024, 20480], P('cont', 'net'), may hold values from -4 to 4
- lam_to: float32 [1024, 20480], P('cont', 'net'), may hold values from -4 to 4
- gen_dual: float32 [1024, 16384], P('cont', 'net'), may hold values from -6 to 6
- base_prev: float32 [16384], P('net'), may hold values from 0 to 0.5
- outage: int32 [1024, 20480], P('cont', 'net'), may hold values 0 or 1
- from_bus: int32 [20480], P('net'), may hold values from 0 to 511
- to_ref: int32 [20480], P('net'), may hold values from 0 to 639, as said below
- halo_rows: int32 [4096], P('net'), may hold values from 0 to 512, as said below
- stiffness: float32 [20480], P('net'), may hold values from 0.5 to 8
- bus_load: float32 [16384], P('net'), may hold values from -3 to 3
- gen_cost: float32 [16384], P('net'), may hold values from 0.25 to 4
- gen_limit: float32 [16384], P('net'), may hold values from 0.05 to 0.6
Outputs:
- angle_field: float32 [1024, 16384], P('cont', 'net')
- generation: float32 [1024, 16384], P('cont', 'net')
- base_setpoint: float32 [16384], P('net')
The draws below stay inside these ranges and needn't reach their ends.
Inputs may be any that keep to these rules, and one draw needn't show every extreme that they name: `halo_rows`: in each partition's 128 entries the live rows come first and are distinct buses of that partition, the rest equal 512; the first partition has no live entry; some partition has all 128 entries live, the others at least half. `to_ref`: A value below 512 is a bus of the branch's own partition; 512 + s names live slot s of the next partition's list; branches of the last partition are all local.
All inputs are finite; a program needn't handle non-finite values. No bound on the sum of `outage` on one device may be relied on, other than what follows from the above.
Results may differ from the reference program's by a relative error of at most 0.0001.
Values sent between devices are 32-bit elements; how exact they have to be, the bound alone decides.
A program may use at most 64 MiB of HBM per device.

```python
import math
import jax
import jax.numpy as jnp

B_DEV = 512
HALO = 128
ROUNDS = 4
BR_DEV = 640
CONTS = 1024
NB = 16384
NBR = 20480
N_NET = 32


def halo_layout(key):
    key_list = jax.random.split(jax.random.fold_in(key, 31), 6)
    index_net = jnp.arange(N_NET, dtype=jnp.int32)
    counts = jax.random.randint(key_list[0], (N_NET,), HALO // 2, HALO + 1)
    fullest = jax.random.randint(key_list[1], (), 1, N_NET)
    counts = jnp.where(index_net == fullest, HALO, counts)
    counts = jnp.where(index_net == 0, 0, counts)
    scores = jax.random.randint(key_list[2], (N_NET, B_DEV), 0, 1 << 18) * B_DEV + jnp.arange(B_DEV, dtype=jnp.int32)[None, :]
    ranked = jnp.argsort(scores, axis=1, stable=True)[:, :HALO].astype(jnp.int32)
    slot_ids = jnp.arange(HALO, dtype=jnp.int32)
    halo_list = jnp.where(slot_ids[None, :] < counts[:, None], ranked, B_DEV).reshape(-1)
    branch = jnp.arange(NBR, dtype=jnp.int32)
    owner = branch // BR_DEV
    remote = (jax.random.randint(key_list[3], (NBR,), 0, 8) < 3) & (owner < N_NET - 1)
    next_part = jnp.minimum(owner + 1, N_NET - 1)
    slot_index = jax.random.randint(key_list[4], (NBR,), 0, HALO) % jnp.maximum(counts[next_part], 1)
    local_bus = jax.random.randint(key_list[5], (NBR,), 0, B_DEV)
    targets = jnp.where(remote, B_DEV + slot_index, local_bus)
    return (halo_list.astype(jnp.int32), targets.astype(jnp.int32))


def draw_halo_rows(key, part):
    return halo_layout(key)[0]


def draw_to_ref(key, part):
    return halo_layout(key)[1]


def set_ends(drawn, rng, smallest, top_value):
    longest = drawn.shape.index(max(drawn.shape))
    spots = []
    for shift in (0, 1):
        where = [jax.random.randint(jax.random.fold_in(rng, axis), (), 0, length) for axis, length in enumerate(drawn.shape)]
        where[longest] = (where[longest] + shift) % drawn.shape[longest]
        spots.append(tuple(where))
    return drawn.at[spots[0]].set(smallest).at[spots[1]].set(top_value)


def shard_levels(rng, extent, shards, smallest, high):
    loudness = 1.0
    for dim, parts in shards:
        heights = jax.random.uniform(jax.random.fold_in(jax.random.fold_in(rng, 6), dim), (parts,), jnp.float32, smallest / len(shards), high / len(shards))
        loudness = loudness * jnp.repeat(jnp.exp(heights), extent[dim] // parts).reshape((-1,) + (1,) * (len(extent) - 1 - dim))
    return loudness


def normal_values(rng, extent, scale, limit, pieces=(), kind=jnp.bfloat16):
    result = scale * jax.random.normal(rng, extent, jnp.float32)
    if pieces:
        result = result * shard_levels(rng, extent, pieces, -0.22, 0.18)
    return jnp.clip(result, -limit, limit).astype(kind)


def setup_inputs(seed: int = 0) -> dict:
    keys = jax.random.split(jax.random.key(seed), 14)
    angles = normal_values(keys[0], (CONTS, NB), 1.0, 6.0, ((0, 16), (1, 32)), jnp.float32)
    lam_from = normal_values(keys[1], (CONTS, NBR), 0.5, 4.0, ((0, 16), (1, 32)), jnp.float32)
    lam_to = normal_values(keys[2], (CONTS, NBR), 0.5, 4.0, ((0, 16), (1, 32)), jnp.float32)
    gen_dual = normal_values(keys[3], (CONTS, NB), 1.0, 6.0, ((0, 16), (1, 32)), jnp.float32)
    base_prev = jnp.clip(0.5 * jax.random.uniform(keys[4], (NB,), jnp.float32) ** shard_levels(keys[4], (NB,), ((0, 32),), -0.2, 0.2), 0.0, 0.5)
    outage = set_ends((jax.random.randint(keys[5], (CONTS, NBR), 0, 8) < 1).astype(jnp.int32), jax.random.fold_in(keys[5], 1), 0, 1)
    from_bus = set_ends(jax.random.randint(keys[6], (NBR,), 0, B_DEV), jax.random.fold_in(keys[6], 1), 0, B_DEV - 1).astype(jnp.int32)
    to_ref = draw_to_ref(jax.random.fold_in(keys[13], 71), 0)
    halo_rows = draw_halo_rows(jax.random.fold_in(keys[13], 71), 0)
    stiffness = jnp.clip(jnp.exp(math.log(8.0) - 2.7725887 * jax.random.uniform(keys[9], (NBR,), jnp.float32) ** shard_levels(keys[9], (NBR,), ((0, 32),), -0.2, 0.2)), 0.5, 8.0)
    bus_load = normal_values(keys[10], (NB,), 0.5, 3.0, ((0, 32),), jnp.float32)
    gen_cost = jnp.clip(jnp.exp(math.log(4.0) - 2.7725887 * jax.random.uniform(keys[11], (NB,), jnp.float32) ** shard_levels(keys[11], (NB,), ((0, 32),), -0.2, 0.2)), 0.25, 4.0)
    gen_limit = jnp.clip(0.05 + 0.55 * jax.random.uniform(keys[12], (NB,), jnp.float32) ** shard_levels(keys[12], (NB,), ((0, 32),), -0.2, 0.2), 0.05, 0.6)
    return dict(angles=angles, lam_from=lam_from, lam_to=lam_to, gen_dual=gen_dual, base_prev=base_prev, outage=outage, from_bus=from_bus, to_ref=to_ref, halo_rows=halo_rows, stiffness=stiffness, bus_load=bus_load, gen_cost=gen_cost, gen_limit=gen_limit)


penalty = 1.0
balance = 2.0


def endpoints(from_bus, to_ref, halo_rows):
    owner = jnp.arange(NBR, dtype=jnp.int32) // BR_DEV
    from_global = owner * B_DEV + from_bus
    next_part = jnp.minimum(owner + 1, N_NET - 1)
    slot_index = jnp.clip(to_ref - B_DEV, 0, HALO - 1)
    remote_row = halo_rows[next_part * HALO + slot_index]
    to_global = jnp.where(to_ref < B_DEV, owner * B_DEV + to_ref, (owner + 1) * B_DEV + remote_row)
    to_global = jnp.clip(to_global, 0, NB - 1).astype(jnp.int32)
    return from_global.astype(jnp.int32), to_global


def reference(angles, lam_from, lam_to, gen_dual, base_prev, outage, from_bus, to_ref, halo_rows, stiffness, bus_load, gen_cost, gen_limit):
    from_global, to_global = endpoints(from_bus, to_ref, halo_rows)
    weighted = stiffness[None, :] * (1.0 - outage.astype(jnp.float32))
    degree = jnp.zeros((NB,), jnp.float32).at[from_global].add(1.0).at[to_global].add(1.0)
    theta = angles
    base_set = base_prev
    copy_from = jnp.zeros_like(lam_from)
    copy_to = jnp.zeros_like(lam_to)
    generation = jnp.zeros_like(gen_dual)
    for round_index in range(ROUNDS):
        if round_index > 0:
            lam_from = lam_from + penalty * (copy_from - theta[:, from_global])
            lam_to = lam_to + penalty * (copy_to - theta[:, to_global])
        target_from = theta[:, from_global] - lam_from / penalty
        target_to = theta[:, to_global] - lam_to / penalty
        angle_gap = penalty * (target_from - target_to) / (penalty + 2.0 * weighted)
        centre = 0.5 * (target_from + target_to)
        copy_from = centre + 0.5 * angle_gap
        copy_to = centre - 0.5 * angle_gap
        branch_flow = weighted * angle_gap
        zeros_field = jnp.zeros((CONTS, NB), jnp.float32)
        copy_sum = zeros_field.at[:, from_global].add(copy_from + lam_from / penalty).at[:, to_global].add(copy_to + lam_to / penalty)
        net_out = zeros_field.at[:, from_global].add(branch_flow).at[:, to_global].add(-branch_flow)
        theta = copy_sum / (degree + 1.0)[None, :]
        generation = (penalty * base_set[None, :] - gen_dual + balance * (bus_load[None, :] + net_out)) / (gen_cost + penalty + balance)[None, :]
        gen_dual = gen_dual + penalty * (generation - base_set[None, :])
        total = jnp.sum(generation + gen_dual / penalty, axis=0)
        base_set = jnp.clip(total / CONTS, 0.0, gen_limit)
    return theta, generation, base_set
```

```python
import functools

import jax
import jax.numpy as jnp
from jax import lax
from jax.experimental import pallas as pl
from jax.experimental.pallas import tpu as pltpu
from jax.sharding import PartitionSpec as P

ROUNDS = 4
LANES = 128
penalty = 1.0
balance = 2.0
F32 = jnp.float32
BF16 = jnp.bfloat16
MESH = pl.DeviceIdType.MESH


def pieces(x):
    high = x.astype(BF16)
    low = (x - high.astype(F32)).astype(BF16)
    return jnp.concatenate([high, low], axis=0)


def fold(y):
    half = y.shape[0] // 2
    return y[:half] + y[half:]


def times(x2, table):
    return fold(jnp.dot(x2, table, preferred_element_type=F32))


def times_t(x2, table):
    return fold(
        lax.dot_general(x2, table, (((1,), (1,)), ((), ())), preferred_element_type=F32)
    )


def is_at(a, b):
    return jnp.where(a == b, 1.0, 0.0).astype(F32)


def kernel(
    n_cont,
    n_net,
    angles_h,
    lam_f_h,
    lam_t_h,
    dual_h,
    outage_h,
    from_h,
    to_h,
    rows_h,
    stiff_h,
    base_h,
    load_h,
    cost_h,
    limit_h,
    theta_o,
    gen_o,
    base_o,
    theta,
    lam_f,
    lam_t,
    dual,
    outage,
    from_v,
    to_v,
    rows_v,
    stiff,
    base_v,
    load,
    cost,
    limit,
    own,
    count,
    edge,
    edge_count,
    listed,
    first_left,
    first_right,
    in_right0,
    in_left0,
    out_left,
    out_right,
    in_left,
    in_right,
    c_out,
    c_in,
    theta_s,
    gen_s,
    base_s,
    in_sem,
    out_sem,
    first_send,
    first_recv,
    send_l,
    recv_l,
    send_r,
    recv_r,
    c_send,
    c_recv,
):
    conts, buses = theta.shape
    branches = lam_f.shape[1]
    slots = rows_v.shape[1]
    me = lax.axis_index("cont")
    part = lax.axis_index("net")
    has_left = part > 0
    has_right = part < n_net - 1

    loads = []
    for i, (src, dst) in enumerate(
        [
            (rows_h, rows_v),
            (from_h, from_v),
            (to_h, to_v),
            (angles_h, theta),
            (lam_f_h, lam_f),
            (lam_t_h, lam_t),
            (outage_h, outage),
            (stiff_h, stiff),
            (dual_h, dual),
            (base_h, base_v),
            (load_h, load),
            (cost_h, cost),
            (limit_h, limit),
        ]
    ):
        copy = pltpu.make_async_copy(src, dst, in_sem.at[i])
        copy.start()
        loads.append(copy)

    in_right0[...] = jnp.zeros_like(in_right0)
    in_left0[...] = jnp.zeros_like(in_left0)
    in_left[...] = jnp.zeros_like(in_left)
    in_right[...] = jnp.zeros_like(in_right)

    barrier = pltpu.get_barrier_semaphore()

    @pl.when(has_left)
    def _():
        pl.semaphore_signal(
            barrier, inc=1, device_id={"cont": me, "net": part - 1}, device_id_type=MESH
        )

    @pl.when(has_right)
    def _():
        pl.semaphore_signal(
            barrier, inc=1, device_id={"cont": me, "net": part + 1}, device_id_type=MESH
        )

    for j in range(1, n_cont):
        pl.semaphore_signal(
            barrier,
            inc=1,
            device_id={"cont": lax.rem(me + j, n_cont), "net": part},
            device_id_type=MESH,
        )

    for copy in loads[:3]:
        copy.wait()
    rows = rows_v[...]
    rows = jnp.where(rows < buses, rows, -1)
    rows_c = jnp.transpose(jnp.broadcast_to(rows.astype(F32), (slots, slots))).astype(jnp.int32)
    lane = lax.broadcasted_iota(jnp.int32, (slots, LANES), 1)
    slot_id = lax.broadcasted_iota(jnp.int32, (slots, LANES), 0)
    for j in range(buses // LANES):
        listed[:, j * LANES : (j + 1) * LANES] = is_at(rows_c, lane + j * LANES).astype(BF16)
    for j in range(branches // LANES):
        cols = slice(j * LANES, (j + 1) * LANES)
        start = from_v[j : j + 1, :]
        end = to_v[j : j + 1, :]
        a, b = is_at(rows_c, start), is_at(rows_c, end)
        edge[:slots, cols] = (a - b).astype(BF16)
        edge_count[:slots, cols] = (a + b).astype(BF16)
        c = is_at(slot_id + buses, end)
        edge[slots:, cols] = (-c).astype(BF16)
        edge_count[slots:, cols] = c.astype(BF16)

    ones = jnp.ones((16, branches), BF16)
    counts = lax.dot_general(
        ones, edge_count[...], (((1,), (1,)), ((), ())), preferred_element_type=F32
    )
    listed_count, slot_count = counts[:, :slots], counts[:, slots:]
    first_right[...] = slot_count
    first_left[conts:, :] = listed_count
    loads[3].wait()
    theta0 = theta[...]
    theta2 = pieces(theta0)
    first_left[:conts, :] = times_t(theta2, listed[...])

    def to_left(src, dst, s, r):
        return pltpu.make_async_remote_copy(
            src, dst, s, r, device_id={"cont": me, "net": part - 1}, device_id_type=MESH
        )

    def to_right(src, dst, s, r):
        return pltpu.make_async_remote_copy(
            src, dst, s, r, device_id={"cont": me, "net": part + 1}, device_id_type=MESH
        )

    first_l = to_left(first_left, in_right0, first_send.at[0], first_recv.at[0])
    first_r = to_right(first_right, in_left0, first_send.at[1], first_recv.at[1])

    inner = has_left & has_right

    @pl.when(inner)
    def _():
        pl.semaphore_wait(barrier, n_cont + 1)

    @pl.when(jnp.logical_not(inner))
    def _():
        pl.semaphore_wait(barrier, n_cont)

    @pl.when(has_left)
    def _():
        first_l.start()

    @pl.when(has_right)
    def _():
        first_r.start()

    bus_id = lax.broadcasted_iota(jnp.int32, (buses, LANES), 0)
    for j in range(branches // LANES):
        cols = slice(j * LANES, (j + 1) * LANES)
        a = is_at(bus_id, from_v[j : j + 1, :])
        b = is_at(bus_id, to_v[j : j + 1, :])
        own[:, cols] = (a - b).astype(BF16)
        count[:, cols] = (a + b).astype(BF16)
    delta = times(theta2, own[...])
    own_count = lax.dot_general(
        ones, count[...], (((1,), (1,)), ((), ())), preferred_element_type=F32
    )[:1]

    for copy in loads[4:]:
        copy.wait()
    share = []
    for j in range(branches // LANES):
        cols = slice(j * LANES, (j + 1) * LANES)
        full = stiff[j : j + 1, :]
        full = full / (penalty + 2.0 * full)
        share.append(full * (1.0 - outage[:, cols].astype(F32)))
    share = jnp.concatenate(share, axis=1)
    lam_gap = lam_f[...] - lam_t[...]

    inv_cost = 1.0 / (cost[...] + (penalty + balance))
    blocks = buses // LANES
    dual_part = dual[...]
    dual_sum = jnp.sum(dual_part, axis=0, keepdims=True)
    inv_row = jnp.concatenate([inv_cost[j : j + 1, :] for j in range(blocks)], axis=1)
    for j in range(blocks):
        c_out[0, blocks + j : blocks + j + 1, :] = dual_sum[:, j * LANES : (j + 1) * LANES]
    for r in range(1, ROUNDS):
        c_out[r, blocks:, :] = jnp.zeros((8 - blocks, LANES), F32)

    @pl.when(has_right)
    def _():
        first_l.wait_recv()

    @pl.when(has_left)
    def _():
        first_r.wait_recv()

    halo = in_right0[:conts, :]
    inv_halo = 1.0 / (in_right0[conts : conts + 1, :] + slot_count[:1] + 1.0)
    keep_halo = 1.0 - inv_halo
    left_count = in_left0[...]
    inv_listed = 1.0 / (listed_count[:1] + left_count[:1] + 1.0)
    degree = own_count + times(pieces(left_count), listed[...])[:1]
    inv_degree = 1.0 / (degree + 1.0)
    keep = 1.0 - inv_degree

    delta = delta + times(pieces(halo), edge[slots:, :])
    flow = share * (delta - lam_gap)
    now = theta0
    for r in range(ROUNDS):
        last = r == ROUNDS - 1
        flow2 = pieces(flow)
        sent = times_t(flow2, edge[...])
        slot_net = sent[:, slots:]
        out_right[r] = slot_net
        copy_r = to_right(out_right.at[r], in_left.at[r], send_r.at[r], recv_r.at[r])

        @pl.when(has_right)
        def _():
            copy_r.start()

        if not last:
            out_left[r] = sent[:, :slots]
            copy_l = to_left(out_left.at[r], in_right.at[r], send_l.at[r], recv_l.at[r])

            @pl.when(has_left)
            def _():
                copy_l.start()

        net = times_t(flow2, own[...])
        now = keep * now - net * inv_degree
        if not last:
            rest = 2.0 * times(pieces(now), own[...]) + (2.0 * flow - delta)

        @pl.when(has_left)
        def _():
            copy_r.wait_recv()

        if not last:

            @pl.when(has_right)
            def _():
                copy_l.wait_recv()

        left = in_left[r]
        if not last:
            halo = keep_halo * halo - (in_right[r] + slot_net) * inv_halo
            arrived = jnp.concatenate([-left * inv_listed, halo], axis=1)
            added = times(pieces(arrived), edge[...])
            gap = rest + 2.0 * added
            new_delta = 0.5 * (gap + delta) - flow
            flow = share * gap
            delta = new_delta

        spread = times(pieces(left), listed[...])
        net = net + spread
        now = now - spread * inv_degree
        if last:
            theta_s[...] = now
            pltpu.make_async_copy(theta_s, theta_o, out_sem.at[0]).start()
        net_sum = jnp.sum(net, axis=0, keepdims=True)
        for j in range(blocks):
            c_out[r, j : j + 1, :] = net_sum[:, j * LANES : (j + 1) * LANES]
        c_in[r, me] = c_out[r]
        for j in range(1, n_cont):
            pltpu.make_async_remote_copy(
                c_out.at[r],
                c_in.at[r, me],
                c_send.at[r],
                c_recv.at[r],
                device_id={"cont": lax.rem(me + j, n_cont), "net": part},
                device_id_type=MESH,
            ).start()
        if not last:
            dual_part = dual_part - (dual_part - 2.0 * net) * inv_row

    def arrived_sum(r):
        pltpu.make_async_copy(
            c_in.at[r, pl.ds(0, n_cont - 1)], c_in.at[r, pl.ds(0, n_cont - 1)], c_recv.at[r]
        ).wait()
        return jnp.sum(c_in[r], axis=0) * (1.0 / (n_cont * conts))

    x = base_v[...]
    loads_now = load[...]
    limits = limit[...]
    beta = jnp.zeros_like(x)
    mean_dual = None
    for r in range(ROUNDS):
        if r == ROUNDS - 1:
            row = (x - beta + balance * loads_now) * inv_cost
            part_gen = (balance * net - dual_part) * inv_row
            for j in range(blocks):
                cols = slice(j * LANES, (j + 1) * LANES)
                gen_s[:, cols] = part_gen[:, cols] + row[j : j + 1, :]
            pltpu.make_async_copy(gen_s, gen_o, out_sem.at[1]).start()
        mean = arrived_sum(r)
        if r == 0:
            mean_dual = mean[blocks:]
        mean_gen = (x - mean_dual + balance * (loads_now + mean[:blocks])) * inv_cost
        mean_dual = mean_dual + (mean_gen - x)
        beta = beta + (x + balance * loads_now - beta) * inv_cost - x
        x = jnp.clip(mean_gen + mean_dual, 0.0, limits)
    base_s[...] = x
    pltpu.make_async_copy(base_s, base_o, out_sem.at[2]).start()

    @pl.when(has_left)
    def _():
        first_l.wait_send()
        for r in range(ROUNDS - 1):
            to_left(out_left.at[r], in_right.at[r], send_l.at[r], recv_l.at[r]).wait_send()

    @pl.when(has_right)
    def _():
        first_r.wait_send()
        for r in range(ROUNDS):
            to_right(out_right.at[r], in_left.at[r], send_r.at[r], recv_r.at[r]).wait_send()

    for r in range(ROUNDS):
        pltpu.make_async_copy(
            c_in.at[r, pl.ds(0, n_cont - 1)], c_in.at[r, pl.ds(0, n_cont - 1)], c_send.at[r]
        ).wait()
    pltpu.make_async_copy(theta_s, theta_o, out_sem.at[0]).wait()
    pltpu.make_async_copy(gen_s, gen_o, out_sem.at[1]).wait()
    pltpu.make_async_copy(base_s, base_o, out_sem.at[2]).wait()


def local(
    n_cont,
    n_net,
    angles,
    lam_from,
    lam_to,
    gen_dual,
    base_prev,
    outage,
    from_bus,
    to_ref,
    halo_rows,
    stiffness,
    bus_load,
    gen_cost,
    gen_limit,
):
    conts, buses = angles.shape
    branches = from_bus.shape[0]
    slots = halo_rows.shape[0]
    blocks = buses // LANES

    def by_lanes(v):
        return v.reshape(v.shape[0] // LANES, LANES)

    anywhere = pl.BlockSpec(memory_space=pl.ANY)
    dma = pltpu.SemaphoreType.DMA
    vmem = pltpu.VMEM
    i32 = jnp.int32
    theta, generation, base = pl.pallas_call(
        functools.partial(kernel, n_cont, n_net),
        out_shape=(
            jax.ShapeDtypeStruct((conts, buses), F32),
            jax.ShapeDtypeStruct((conts, buses), F32),
            jax.ShapeDtypeStruct((blocks, LANES), F32),
        ),
        in_specs=[anywhere] * 13,
        out_specs=(anywhere,) * 3,
        scratch_shapes=[
            vmem((conts, buses), F32),
            vmem((conts, branches), F32),
            vmem((conts, branches), F32),
            vmem((conts, buses), F32),
            vmem((conts, branches), i32),
            vmem((branches // LANES, LANES), i32),
            vmem((branches // LANES, LANES), i32),
            vmem((1, slots), i32),
            vmem((branches // LANES, LANES), F32),
            vmem((blocks, LANES), F32),
            vmem((blocks, LANES), F32),
            vmem((blocks, LANES), F32),
            vmem((blocks, LANES), F32),
            vmem((buses, branches), BF16),
            vmem((buses, branches), BF16),
            vmem((2 * slots, branches), BF16),
            vmem((2 * slots, branches), BF16),
            vmem((slots, buses), BF16),
            vmem((conts + 16, slots), F32),
            vmem((16, slots), F32),
            vmem((conts + 16, slots), F32),
            vmem((16, slots), F32),
            vmem((ROUNDS, conts, slots), F32),
            vmem((ROUNDS, conts, slots), F32),
            vmem((ROUNDS, conts, slots), F32),
            vmem((ROUNDS, conts, slots), F32),
            vmem((ROUNDS, 8, LANES), F32),
            vmem((ROUNDS, n_cont, 8, LANES), F32),
            vmem((conts, buses), F32),
            vmem((conts, buses), F32),
            vmem((blocks, LANES), F32),
            dma((13,)),
            dma((3,)),
            dma((2,)),
            dma((2,)),
            dma((ROUNDS,)),
            dma((ROUNDS,)),
            dma((ROUNDS,)),
            dma((ROUNDS,)),
            dma((ROUNDS,)),
            dma((ROUNDS,)),
        ],
        compiler_params=pltpu.CompilerParams(collective_id=0, has_side_effects=True),
        name="rounds",
    )(
        angles,
        lam_from,
        lam_to,
        gen_dual,
        outage,
        by_lanes(from_bus),
        by_lanes(to_ref),
        by_lanes(halo_rows),
        by_lanes(stiffness),
        by_lanes(base_prev),
        by_lanes(bus_load),
        by_lanes(gen_cost),
        by_lanes(gen_limit),
    )
    return theta, generation, base.reshape(buses)


def solution(mesh):
    both = P("cont", "net")
    one = P("net")
    placed = (both, both, both, both, one, both, one, one, one, one, one, one, one)
    return jax.shard_map(
        functools.partial(local, mesh.shape["cont"], mesh.shape["net"]),
        mesh=mesh,
        in_specs=placed,
        out_specs=(both, both, one),
        check_vma=False,
    )
```

```python
import functools

import jax
import jax.numpy as jnp
from jax import lax
from jax.experimental import pallas as pl
from jax.experimental.pallas import tpu as pltpu
from jax.sharding import PartitionSpec as P

ROUNDS = 4
LANES = 128
penalty = 1.0
balance = 2.0
F32 = jnp.float32
BF16 = jnp.bfloat16
MESH = pl.DeviceIdType.MESH


def pieces(x):
    high = x.astype(BF16)
    low = (x - high.astype(F32)).astype(BF16)
    return jnp.concatenate([high, low], axis=0)


def fold(y):
    half = y.shape[0] // 2
    return y[:half] + y[half:]


def times(x2, table):
    return fold(jnp.dot(x2, table, preferred_element_type=F32))


def times_t(x2, table):
    return fold(
        lax.dot_general(x2, table, (((1,), (1,)), ((), ())), preferred_element_type=F32)
    )


def times3(x, table):
    high = x.astype(BF16)
    rest = x - high.astype(F32)
    y = fold(jnp.dot(pieces(rest), table, preferred_element_type=F32))
    return y + jnp.dot(high, table, preferred_element_type=F32)


def is_at(a, b):
    return jnp.where(a == b, 1.0, 0.0).astype(F32)


def kernel(
    n_cont,
    n_net,
    row,
    angles_h,
    lam_f_h,
    lam_t_h,
    dual_h,
    outage_h,
    from_h,
    to_h,
    rows_h,
    stiff_h,
    base_h,
    load_h,
    cost_h,
    limit_h,
    theta_o,
    gen_o,
    base_o,
    theta,
    lam_f,
    lam_t,
    dual,
    outage,
    from_v,
    to_v,
    rows_v,
    stiff,
    base_v,
    load,
    cost,
    limit,
    own,
    count,
    edge,
    edge_count,
    listed,
    pick_out,
    pick_in,
    count_out,
    count_in,
    out_left,
    out_right,
    in_left,
    in_right,
    first_out,
    first_in,
    c_out,
    c_in,
    slot_out,
    slot_in,
    in_sem,
    pick_sem,
    count_send,
    count_recv,
    send_l,
    recv_l,
    send_r,
    recv_r,
    c_send,
    c_recv,
    slot_sem,
    plane_sem,
    next_sem,
):
    conts, buses = theta.shape
    branches = lam_f.shape[1]
    slots = rows_v.shape[1]
    blocks = buses // LANES
    me = lax.axis_index("cont")
    part = lax.axis_index("net")
    has_left = part > 0
    has_right = part < n_net - 1
    my_row, my_col = me // row, lax.rem(me, row)
    n_rows = n_cont // row

    def at(c, p):
        return dict(device_id={"cont": c, "net": p}, device_id_type=MESH)

    loads = []
    for i, (src, dst) in enumerate(
        [
            (rows_h, rows_v),
            (angles_h, theta),
            (from_h, from_v),
            (to_h, to_v),
            (lam_f_h, lam_f),
            (lam_t_h, lam_t),
            (outage_h, outage),
            (stiff_h, stiff),
            (dual_h, dual),
            (base_h, base_v),
            (load_h, load),
            (cost_h, cost),
            (limit_h, limit),
        ]
    ):
        copy = pltpu.make_async_copy(src, dst, in_sem.at[i])
        copy.start()
        loads.append(copy)

    @pl.when(jnp.logical_not(has_left))
    def _():
        count_in[0] = jnp.zeros((8, slots), F32)
        in_left[...] = jnp.zeros_like(in_left)
        slot_in[...] = jnp.zeros_like(slot_in)

    @pl.when(jnp.logical_not(has_right))
    def _():
        count_in[1] = jnp.zeros((8, slots), F32)
        pick_in[...] = jnp.zeros_like(pick_in)
        in_right[...] = jnp.zeros_like(in_right)

    barrier = pltpu.get_barrier_semaphore()
    column = [lax.rem(my_row + j, n_rows) * row + my_col for j in range(1, n_rows)]
    near = [my_row * row + lax.rem(my_col + j, row) for j in range(1, row)] + column

    @pl.when(has_left)
    def _():
        pl.semaphore_signal(barrier, inc=1, **at(me, part - 1))

    @pl.when(has_right)
    def _():
        pl.semaphore_signal(barrier, inc=1, **at(me, part + 1))

    for c in near:
        pl.semaphore_signal(barrier, inc=1, **at(c, part))

    loads[0].wait()
    rows = rows_v[...]
    rows = jnp.where(rows < buses, rows, -1)
    rows_c = jnp.transpose(jnp.broadcast_to(rows.astype(F32), (slots, slots))).astype(jnp.int32)
    lane = lax.broadcasted_iota(jnp.int32, (slots, LANES), 1)
    slot_id = lax.broadcasted_iota(jnp.int32, (slots, LANES), 0)
    for j in range(blocks):
        listed[:, j * LANES : (j + 1) * LANES] = is_at(rows_c, lane + j * LANES).astype(BF16)
    loads[1].wait()
    theta0 = theta[...]
    theta2 = pieces(theta0)
    pick_out[...] = times_t(theta2, listed[...])

    inner = has_left & has_right

    @pl.when(inner)
    def _():
        pl.semaphore_wait(barrier, len(near) + 2)

    @pl.when(jnp.logical_not(inner))
    def _():
        pl.semaphore_wait(barrier, len(near) + 1)

    def to_left(src, dst, s, r):
        return pltpu.make_async_remote_copy(src, dst, s, r, **at(me, part - 1))

    def to_right(src, dst, s, r):
        return pltpu.make_async_remote_copy(src, dst, s, r, **at(me, part + 1))

    pick = to_left(pick_out, pick_in, pick_sem.at[0], pick_sem.at[1])

    @pl.when(has_left)
    def _():
        pick.start()

    for c in column:
        pl.semaphore_signal(plane_sem, inc=1, **at(c, part))

    loads[2].wait()
    loads[3].wait()
    for j in range(branches // LANES):
        cols = slice(j * LANES, (j + 1) * LANES)
        start = from_v[j : j + 1, :]
        end = to_v[j : j + 1, :]
        a, b = is_at(rows_c, start), is_at(rows_c, end)
        edge[:slots, cols] = (a - b).astype(BF16)
        edge_count[:slots, cols] = (a + b).astype(BF16)
        c = is_at(slot_id + buses, end)
        edge[slots:, cols] = (-c).astype(BF16)
        edge_count[slots:, cols] = c.astype(BF16)

    ones = jnp.ones((16, branches), BF16)
    counts = lax.dot_general(
        ones, edge_count[...], (((1,), (1,)), ((), ())), preferred_element_type=F32
    )
    listed_count, slot_count = counts[:8, :slots], counts[:8, slots:]
    count_out[0] = listed_count
    count_out[1] = slot_count
    count_l = to_left(count_out.at[0], count_in.at[1], count_send.at[0], count_recv.at[0])
    count_r = to_right(count_out.at[1], count_in.at[0], count_send.at[1], count_recv.at[1])

    @pl.when(has_left)
    def _():
        count_l.start()

    @pl.when(has_right)
    def _():
        count_r.start()

    bus_id = lax.broadcasted_iota(jnp.int32, (buses, LANES), 0)
    for j in range(branches // LANES):
        cols = slice(j * LANES, (j + 1) * LANES)
        a = is_at(bus_id, from_v[j : j + 1, :])
        b = is_at(bus_id, to_v[j : j + 1, :])
        own[:, cols] = (a - b).astype(BF16)
        count[:, cols] = (a + b).astype(BF16)
    delta = times(theta2, own[...])

    for copy in loads[4:]:
        copy.wait()
    share = []
    for j in range(branches // LANES):
        cols = slice(j * LANES, (j + 1) * LANES)
        full = stiff[j : j + 1, :]
        full = full / (penalty + 2.0 * full)
        share.append(full * (1.0 - outage[:, cols].astype(F32)))
    share = jnp.concatenate(share, axis=1)
    lam_gap = lam_f[...] - lam_t[...]

    own_count = lax.dot_general(
        ones, count[...], (((1,), (1,)), ((), ())), preferred_element_type=F32
    )[:1]
    inv_cost = 1.0 / (cost[...] + (penalty + balance))
    dual_part = dual[...]
    dual_sum = jnp.sum(dual_part, axis=0, keepdims=True)
    inv_row = jnp.concatenate([inv_cost[j : j + 1, :] for j in range(blocks)], axis=1)
    for j in range(blocks):
        first_out[blocks + j : blocks + j + 1, :] = dual_sum[:, j * LANES : (j + 1) * LANES]

    @pl.when(has_right)
    def _():
        pick.wait_recv()

    halo = pick_in[...]
    delta = delta + times(pieces(halo), edge[slots:, :])
    flow = share * (delta - lam_gap)
    now = theta0
    net = net_here = None

    def share_sums(src, dst, s, r, sums):
        for j in range(blocks):
            src[j : j + 1, :] = sums[:, j * LANES : (j + 1) * LANES]
        dst[me] = src[...]
        for j in range(1, n_cont):
            pltpu.make_async_remote_copy(
                src, dst.at[me], s, r, **at(lax.rem(me + j, n_cont), part)
            ).start()

    for r in range(ROUNDS):
        last = r == ROUNDS - 1
        flow2 = pieces(flow)
        sent = times_t(flow2, edge[...])
        slot_net = sent[:, slots:]
        out_right[r] = slot_net
        copy_r = to_right(out_right.at[r], in_left.at[r], send_r.at[r], recv_r.at[r])

        @pl.when(has_right)
        def _():
            copy_r.start()

        if not last:
            out_left[r] = sent[:, :slots]
            copy_l = to_left(out_left.at[r], in_right.at[r], send_l.at[r], recv_l.at[r])

            @pl.when(has_left)
            def _():
                copy_l.start()

        net_here = times_t(flow2, own[...])
        if last:
            slot_out[...] = jnp.sum(slot_net, axis=0, keepdims=True)
            share_sums(
                c_out.at[r - 1],
                c_in.at[r - 1],
                c_send.at[r],
                c_recv.at[r],
                jnp.sum(net_here, axis=0, keepdims=True),
            )

            @pl.when(has_right)
            def _():
                pl.semaphore_wait(next_sem, 1)
                for j in range(n_cont):
                    pltpu.make_async_remote_copy(
                        slot_out,
                        slot_in.at[me],
                        slot_sem.at[0],
                        slot_sem.at[1],
                        **at(lax.rem(me + j, n_cont), part + 1),
                    ).start()

        if r == 0:

            @pl.when(has_right)
            def _():
                count_l.wait_recv()

            @pl.when(has_left)
            def _():
                count_r.wait_recv()

            left_count = count_in[0]
            inv_halo = 1.0 / (count_in[1][:1] + slot_count[:1] + 1.0)
            keep_halo = 1.0 - inv_halo
            inv_listed = 1.0 / (listed_count[:1] + left_count[:1] + 1.0)
            left_count = jnp.concatenate([left_count, left_count], axis=0)
            degree = own_count + times(pieces(left_count), listed[...])[:1]
            inv_degree = 1.0 / (degree + 1.0)
            keep = 1.0 - inv_degree
        else:
            spread = times(pieces(left), listed[...])
            net = net + spread
            now = now - spread * inv_degree
            if r == 1:
                pl.semaphore_wait(plane_sem, len(column))

                @pl.when(has_left)
                def _():
                    pl.semaphore_signal(next_sem, inc=1, **at(me, part - 1))

                share_sums(
                    first_out,
                    first_in,
                    c_send.at[0],
                    c_recv.at[0],
                    jnp.sum(net, axis=0, keepdims=True),
                )
            else:
                share_sums(
                    c_out.at[r - 2],
                    c_in.at[r - 2],
                    c_send.at[r - 1],
                    c_recv.at[r - 1],
                    jnp.sum(net, axis=0, keepdims=True),
                )
            dual_part = dual_part - (dual_part - 2.0 * net) * inv_row

        net = net_here
        now = keep * now - net * inv_degree
        if not last:
            rest = 2.0 * times(pieces(now), own[...]) + (2.0 * flow - delta)

        @pl.when(has_left)
        def _():
            copy_r.wait_recv()

        if not last:

            @pl.when(has_right)
            def _():
                copy_l.wait_recv()

        left = in_left[r]
        if not last:
            halo = keep_halo * halo - (in_right[r] + slot_net) * inv_halo
            arrived = jnp.concatenate([-left * inv_listed, halo], axis=1)
            added = times(pieces(arrived), edge[...])
            gap = rest + 2.0 * added
            delta, flow = 0.5 * (gap + delta) - flow, share * gap

    spread = times(pieces(left), listed[...])
    theta_o[...] = now - spread * inv_degree
    net = net + spread

    def taken(ref, sem):
        pltpu.make_async_copy(
            ref.at[pl.ds(0, n_cont - 1)], ref.at[pl.ds(0, n_cont - 1)], sem
        ).wait()

    x = base_v[...]
    loads_now = load[...]
    limits = limit[...]
    beta = jnp.zeros_like(x)
    scale = 1.0 / (n_cont * conts)
    mean_dual = None
    for r in range(ROUNDS):
        last = r == ROUNDS - 1
        if last:
            row_gen = (x - beta + balance * loads_now) * inv_cost
            part_gen = (balance * net - dual_part) * inv_row
            for j in range(blocks):
                cols = slice(j * LANES, (j + 1) * LANES)
                gen_o[:, cols] = part_gen[:, cols] + row_gen[j : j + 1, :]
        taken(first_in if r == 0 else c_in.at[r - 1], c_recv.at[r])
        total = jnp.sum(first_in[...] if r == 0 else c_in[r - 1], axis=0)
        if r == 0:
            mean_dual = total[blocks:] * scale
            total = total[:blocks]
        if last:

            @pl.when(has_left)
            def _():
                pltpu.make_async_copy(slot_in, slot_in, slot_sem.at[1]).wait()

            slot_sum = jnp.broadcast_to(jnp.sum(slot_in[...], axis=0), (16, slots))
            placed = times3(slot_sum, listed[...])
            total = total + jnp.concatenate(
                [placed[:1, j * LANES : (j + 1) * LANES] for j in range(blocks)], axis=0
            )
        mean = total * scale
        mean_gen = (x - mean_dual + balance * (loads_now + mean)) * inv_cost
        mean_dual = mean_dual + (mean_gen - x)
        beta = beta + (x + balance * loads_now - beta) * inv_cost - x
        x = jnp.clip(mean_gen + mean_dual, 0.0, limits)
    base_o[...] = x

    @pl.when(has_left)
    def _():
        pick.wait_send()
        count_l.wait_send()
        for r in range(ROUNDS - 1):
            to_left(out_left.at[r], in_right.at[r], send_l.at[r], recv_l.at[r]).wait_send()

    @pl.when(has_right)
    def _():
        count_r.wait_send()
        for r in range(ROUNDS):
            to_right(out_right.at[r], in_left.at[r], send_r.at[r], recv_r.at[r]).wait_send()
        pltpu.make_async_copy(slot_in, slot_in, slot_sem.at[0]).wait()

    for r in range(ROUNDS):
        taken(first_in if r == 0 else c_in.at[r - 1], c_send.at[r])


def finish(theta, gen, base, theta_o, gen_o, base_o, sem):
    copies = [
        pltpu.make_async_copy(src, dst, sem.at[i])
        for i, (src, dst) in enumerate([(theta, theta_o), (gen, gen_o), (base, base_o)])
    ]
    for copy in copies:
        copy.start()
    for copy in copies:
        copy.wait()


def local(
    n_cont,
    n_net,
    angles,
    lam_from,
    lam_to,
    gen_dual,
    base_prev,
    outage,
    from_bus,
    to_ref,
    halo_rows,
    stiffness,
    bus_load,
    gen_cost,
    gen_limit,
):
    conts, buses = angles.shape
    branches = from_bus.shape[0]
    slots = halo_rows.shape[0]
    blocks = buses // LANES
    row = n_cont
    for r in range(1, n_cont + 1):
        if n_cont % r == 0 and r * r <= n_cont:
            row = r

    def by_lanes(v):
        return v.reshape(v.shape[0] // LANES, LANES)

    inside = pl.BlockSpec(memory_space=pltpu.VMEM)
    outside = pl.BlockSpec(memory_space=pltpu.HBM)
    dma = pltpu.SemaphoreType.DMA
    vmem = pltpu.VMEM
    i32 = jnp.int32
    kept = pl.pallas_call(
        functools.partial(kernel, n_cont, n_net, row),
        out_shape=(
            pltpu.VMEM((conts, buses), F32),
            pltpu.VMEM((conts, buses), F32),
            pltpu.VMEM((blocks, LANES), F32),
        ),
        in_specs=[outside] * 13,
        out_specs=(inside,) * 3,
        scratch_shapes=[
            vmem((conts, buses), F32),
            vmem((conts, branches), F32),
            vmem((conts, branches), F32),
            vmem((conts, buses), F32),
            vmem((conts, branches), i32),
            vmem((branches // LANES, LANES), i32),
            vmem((branches // LANES, LANES), i32),
            vmem((1, slots), i32),
            vmem((branches // LANES, LANES), F32),
            vmem((blocks, LANES), F32),
            vmem((blocks, LANES), F32),
            vmem((blocks, LANES), F32),
            vmem((blocks, LANES), F32),
            vmem((buses, branches), BF16),
            vmem((buses, branches), BF16),
            vmem((2 * slots, branches), BF16),
            vmem((2 * slots, branches), BF16),
            vmem((slots, buses), BF16),
            vmem((conts, slots), F32),
            vmem((conts, slots), F32),
            vmem((2, 8, slots), F32),
            vmem((2, 8, slots), F32),
            vmem((ROUNDS, conts, slots), F32),
            vmem((ROUNDS, conts, slots), F32),
            vmem((ROUNDS, conts, slots), F32),
            vmem((ROUNDS, conts, slots), F32),
            vmem((2 * blocks, LANES), F32),
            vmem((n_cont, 2 * blocks, LANES), F32),
            vmem((ROUNDS - 1, blocks, LANES), F32),
            vmem((ROUNDS - 1, n_cont, blocks, LANES), F32),
            vmem((1, slots), F32),
            vmem((n_cont, 1, slots), F32),
            dma((13,)),
            dma((2,)),
            dma((2,)),
            dma((2,)),
            dma((ROUNDS,)),
            dma((ROUNDS,)),
            dma((ROUNDS,)),
            dma((ROUNDS,)),
            dma((ROUNDS,)),
            dma((ROUNDS,)),
            dma((2,)),
            pltpu.SemaphoreType.REGULAR,
            pltpu.SemaphoreType.REGULAR,
        ],
        compiler_params=pltpu.CompilerParams(
            collective_id=0, has_side_effects=True
        ),
        name="rounds",
    )(
        angles,
        lam_from,
        lam_to,
        gen_dual,
        outage,
        by_lanes(from_bus),
        by_lanes(to_ref),
        by_lanes(halo_rows),
        by_lanes(stiffness),
        by_lanes(base_prev),
        by_lanes(bus_load),
        by_lanes(gen_cost),
        by_lanes(gen_limit),
    )
    theta, generation, base = pl.pallas_call(
        finish,
        out_shape=(
            jax.ShapeDtypeStruct((conts, buses), F32),
            jax.ShapeDtypeStruct((conts, buses), F32),
            jax.ShapeDtypeStruct((blocks, LANES), F32),
        ),
        in_specs=[inside] * 3,
        out_specs=(outside,) * 3,
        scratch_shapes=[dma((3,))],
        compiler_params=pltpu.CompilerParams(vmem_limit_bytes=4 << 20),
        name="finish",
    )(*kept)
    return theta, generation, base.reshape(buses)


def solution(mesh):
    both = P("cont", "net")
    one = P("net")
    placed = (both, both, both, both, one, both, one, one, one, one, one, one, one)
    return jax.shard_map(
        functools.partial(local, mesh.shape["cont"], mesh.shape["net"]),
        mesh=mesh,
        in_specs=placed,
        out_specs=(both, both, one),
        check_vma=False,
    )
```

```python
import functools

import jax
import jax.numpy as jnp
from jax import lax
from jax.experimental import pallas as pl
from jax.experimental.pallas import tpu as pltpu
from jax.sharding import PartitionSpec as P

ROUNDS = 4
LANES = 128
STREAMS = 2
CHUNKS = 4
penalty = 1.0
balance = 2.0
F32 = jnp.float32
BF16 = jnp.bfloat16
MESH = pl.DeviceIdType.MESH


def pieces(x):
    high = x.astype(BF16)
    low = (x - high.astype(F32)).astype(BF16)
    return jnp.concatenate([high, low], axis=0)


def fold(y):
    half = y.shape[0] // 2
    return y[:half] + y[half:]


def times(x2, table):
    return fold(jnp.dot(x2, table, preferred_element_type=F32))


def times_t(x2, table):
    return fold(
        lax.dot_general(x2, table, (((1,), (1,)), ((), ())), preferred_element_type=F32)
    )


def is_at(a, b):
    return jnp.where(a == b, 1.0, 0.0).astype(F32)


def kernel(
    n_cont,
    n_net,
    row,
    angles_h,
    lam_f_h,
    lam_t_h,
    dual_h,
    outage_h,
    from_h,
    to_h,
    rows_h,
    stiff_h,
    base_h,
    load_h,
    cost_h,
    limit_h,
    theta_o,
    gen_o,
    base_o,
    theta,
    lam_f,
    lam_t,
    dual,
    outage,
    from_v,
    to_v,
    rows_v,
    stiff,
    base_v,
    load,
    cost,
    limit,
    own,
    count,
    edge,
    edge_count,
    listed,
    pick_out,
    pick_in,
    count_out,
    count_in,
    out_left,
    out_right,
    in_left,
    in_right,
    c0_out,
    c0_in,
    c_out,
    c_in,
    slot0_out,
    slot0_in,
    slot_out,
    slot_in,
    in_sem,
    pick_sem,
    count_send,
    count_recv,
    send_l,
    recv_l,
    send_r,
    recv_r,
    c_sem,
    slot_sem,
    plane_sem,
    next_sem,
):
    conts, buses = theta.shape
    branches = lam_f.shape[1]
    slots = rows_v.shape[1]
    blocks = buses // LANES
    part_rows = conts // STREAMS
    me = lax.axis_index("cont")
    part = lax.axis_index("net")
    has_left = part > 0
    has_right = part < n_net - 1
    my_row, my_col = lax.div(me, row), lax.rem(me, row)
    n_rows = n_cont // row

    def at(c, p):
        return dict(device_id={"cont": c, "net": p}, device_id_type=MESH)

    loads = []
    for i, (src, dst) in enumerate(
        [
            (rows_h, rows_v),
            (angles_h, theta),
            (from_h, from_v),
            (to_h, to_v),
            (lam_f_h, lam_f),
            (lam_t_h, lam_t),
            (outage_h, outage),
            (stiff_h, stiff),
            (dual_h, dual),
            (base_h, base_v),
            (load_h, load),
            (cost_h, cost),
            (limit_h, limit),
        ]
    ):
        copy = pltpu.make_async_copy(src, dst, in_sem.at[i])
        copy.start()
        loads.append(copy)

    @pl.when(jnp.logical_not(has_left))
    def _():
        count_in[0] = jnp.zeros((8, slots), F32)
        in_left[...] = jnp.zeros_like(in_left)
        slot0_in[...] = jnp.zeros_like(slot0_in)
        slot_in[...] = jnp.zeros_like(slot_in)

    @pl.when(jnp.logical_not(has_right))
    def _():
        count_in[1] = jnp.zeros((8, slots), F32)
        pick_in[...] = jnp.zeros_like(pick_in)
        in_right[...] = jnp.zeros_like(in_right)

    barrier = pltpu.get_barrier_semaphore()
    column = [lax.rem(my_row + j, n_rows) * row + my_col for j in range(1, n_rows)]
    near = [my_row * row + lax.rem(my_col + j, row) for j in range(1, row)] + column

    @pl.when(has_left)
    def _():
        pl.semaphore_signal(barrier, inc=1, **at(me, part - 1))

    @pl.when(has_right)
    def _():
        pl.semaphore_signal(barrier, inc=1, **at(me, part + 1))

    for c in near:
        pl.semaphore_signal(barrier, inc=1, **at(c, part))

    def hops(step):
        return min(step[0], n_rows - step[0]) + min(step[1], row - step[1])

    steps = sorted(((i, j) for i in range(n_rows) for j in range(row)), key=hops, reverse=True)
    plane = [
        lax.rem(my_row + i, n_rows) * row + lax.rem(my_col + j, row) for i, j in steps
    ]

    loads[0].wait()
    rows = rows_v[...]
    rows = jnp.where(rows < buses, rows, -1)
    rows_c = jnp.transpose(jnp.broadcast_to(rows.astype(F32), (slots, slots))).astype(jnp.int32)
    lane = lax.broadcasted_iota(jnp.int32, (slots, LANES), 1)
    slot_id = lax.broadcasted_iota(jnp.int32, (slots, LANES), 0)
    for j in range(blocks):
        listed[:, j * LANES : (j + 1) * LANES] = is_at(rows_c, lane + j * LANES).astype(BF16)
    loads[1].wait()
    theta0 = theta[...]
    theta2 = pieces(theta0)
    picked = times_t(theta2, listed[...])
    for s in range(STREAMS):
        pick_out[s] = picked[s * part_rows : (s + 1) * part_rows]

    inner = has_left & has_right

    @pl.when(inner)
    def _():
        pl.semaphore_wait(barrier, len(near) + 2)

    @pl.when(jnp.logical_not(inner))
    def _():
        pl.semaphore_wait(barrier, len(near) + 1)

    def to_left(src, dst, s, r):
        return pltpu.make_async_remote_copy(src, dst, s, r, **at(me, part - 1))

    def to_right(src, dst, s, r):
        return pltpu.make_async_remote_copy(src, dst, s, r, **at(me, part + 1))

    def pick(s):
        return to_left(pick_out.at[s], pick_in.at[s], pick_sem.at[0, s], pick_sem.at[1, s])

    def left_copy(r, s):
        return to_left(out_left.at[r, s], in_right.at[r, s], send_l.at[r, s], recv_l.at[r, s])

    def right_copy(r, s):
        return to_right(out_right.at[r, s], in_left.at[r, s], send_r.at[r, s], recv_r.at[r, s])

    @pl.when(has_left)
    def _():
        for s in range(STREAMS):
            pick(s).start()

    for c in column:
        pl.semaphore_signal(plane_sem, inc=1, **at(c, part))

    loads[2].wait()
    loads[3].wait()
    for j in range(branches // LANES):
        cols = slice(j * LANES, (j + 1) * LANES)
        start = from_v[j : j + 1, :]
        end = to_v[j : j + 1, :]
        a, b = is_at(rows_c, start), is_at(rows_c, end)
        edge[:slots, cols] = (a - b).astype(BF16)
        edge_count[:slots, cols] = (a + b).astype(BF16)
        c = is_at(slot_id + buses, end)
        edge[slots:, cols] = (-c).astype(BF16)
        edge_count[slots:, cols] = c.astype(BF16)

    ones = jnp.ones((16, branches), BF16)
    counts = lax.dot_general(
        ones, edge_count[...], (((1,), (1,)), ((), ())), preferred_element_type=F32
    )
    listed_count, slot_count = counts[:8, :slots], counts[:8, slots:]
    count_out[0] = listed_count
    count_out[1] = slot_count
    count_l = to_left(count_out.at[0], count_in.at[1], count_send.at[0], count_recv.at[0])
    count_r = to_right(count_out.at[1], count_in.at[0], count_send.at[1], count_recv.at[1])

    @pl.when(has_left)
    def _():
        count_l.start()

    @pl.when(has_right)
    def _():
        count_r.start()

    bus_id = lax.broadcasted_iota(jnp.int32, (buses, LANES), 0)
    for j in range(branches // LANES):
        cols = slice(j * LANES, (j + 1) * LANES)
        a = is_at(bus_id, from_v[j : j + 1, :])
        b = is_at(bus_id, to_v[j : j + 1, :])
        own[:, cols] = (a - b).astype(BF16)
        count[:, cols] = (a + b).astype(BF16)
    delta = times(theta2, own[...])

    for copy in loads[4:]:
        copy.wait()
    share = []
    for j in range(branches // LANES):
        cols = slice(j * LANES, (j + 1) * LANES)
        full = stiff[j : j + 1, :]
        full = full / (penalty + 2.0 * full)
        share.append(full * (1.0 - outage[:, cols].astype(F32)))
    share = jnp.concatenate(share, axis=1)
    rest = delta - (lam_f[...] - lam_t[...])

    own_count = lax.dot_general(
        ones, count[...], (((1,), (1,)), ((), ())), preferred_element_type=F32
    )[:1]
    inv_cost = 1.0 / (cost[...] + (penalty + balance))
    dual_part = dual[...]
    inv_row = jnp.concatenate([inv_cost[j : j + 1, :] for j in range(blocks)], axis=1)

    def store_sums(dst, values):
        sums = jnp.sum(values, axis=0, keepdims=True)
        for j in range(blocks):
            dst[j : j + 1, :] = sums[:, j * LANES : (j + 1) * LANES]

    store_sums(c0_out.at[2], dual_part)

    def across(src, dst, sem):
        dst[me] = src[...]
        for c in plane[:-1]:
            pltpu.make_async_remote_copy(
                src, dst.at[me], sem.at[0], sem.at[1], **at(c, part)
            ).start()

    def onward(src, dst, sem):
        @pl.when(has_right)
        def _():
            for c in plane:
                pltpu.make_async_remote_copy(
                    src, dst.at[me], sem.at[0], sem.at[1], **at(c, part + 1)
                ).start()

    halos = [None] * STREAMS
    slot_nets = [None] * STREAMS
    now = theta0
    net = None
    for r in range(ROUNDS):
        last = r == ROUNDS - 1
        lefts, flows, deltas = [], [], []
        for s in range(STREAMS):
            block = slice(s * part_rows, (s + 1) * part_rows)

            @pl.when(has_right)
            def _():
                if r == 0:
                    pick(s).wait_recv()
                else:
                    left_copy(r - 1, s).wait_recv()

            if r == 0:
                halos[s] = pick_in[s]
                added = times(pieces(halos[s]), edge[slots:, :])
                deltas.append(delta[block] + added)
                flows.append(share[block] * (rest[block] + added))
            else:

                @pl.when(has_left)
                def _():
                    right_copy(r - 1, s).wait_recv()

                left = in_left[r - 1, s]
                lefts.append(left)
                halos[s] = keep_halo * halos[s] - (in_right[r - 1, s] + slot_nets[s]) * inv_halo
                arrived = jnp.concatenate([-left * inv_listed, halos[s]], axis=1)
                gap = rest[block] + 2.0 * times(pieces(arrived), edge[...])
                deltas.append(0.5 * (gap + delta[block]) - flow[block])
                flows.append(share[block] * gap)
            sent = times_t(pieces(flows[s]), edge[...])
            slot_nets[s] = sent[:, slots:]
            out_right[r, s] = slot_nets[s]
            if not last:
                out_left[r, s] = sent[:, :slots]

            @pl.when(has_right)
            def _():
                right_copy(r, s).start()

            if not last:

                @pl.when(has_left)
                def _():
                    left_copy(r, s).start()

        flow = jnp.concatenate(flows, axis=0)
        delta = jnp.concatenate(deltas, axis=0)
        slot_sum = sum(jnp.sum(v, axis=0, keepdims=True) for v in slot_nets)
        if r < 2:
            slot0_out[r : r + 1, :] = slot_sum
        else:
            slot_out[r - 2] = slot_sum
            onward(slot_out.at[r - 2], slot_in.at[r - 2], slot_sem.at[r - 1])
        net_here = times_t(pieces(flow), own[...])
        store_sums(c0_out.at[r] if r < 2 else c_out.at[r - 2], net_here)
        if r >= 2:
            across(c_out.at[r - 2], c_in.at[r - 2], c_sem.at[r - 1])

        if r == 0:

            @pl.when(has_right)
            def _():
                count_l.wait_recv()

            @pl.when(has_left)
            def _():
                count_r.wait_recv()

            left_count = count_in[0]
            inv_halo = 1.0 / (count_in[1][:1] + slot_count[:1] + 1.0)
            keep_halo = 1.0 - inv_halo
            inv_listed = 1.0 / (listed_count[:1] + left_count[:1] + 1.0)
            left_count = jnp.concatenate([left_count, left_count], axis=0)
            degree = own_count + times(pieces(left_count), listed[...])[:1]
            inv_degree = 1.0 / (degree + 1.0)
            keep = 1.0 - inv_degree
        else:
            spread = times(pieces(jnp.concatenate(lefts, axis=0)), listed[...])
            net = net + spread
            now = now - spread * inv_degree
            dual_part = dual_part - (dual_part - 2.0 * net) * inv_row

        net = net_here
        now = keep * now - net * inv_degree
        if not last:
            rest = 2.0 * times(pieces(now), own[...]) + (2.0 * flow - delta)
        if r == 0:
            pl.semaphore_wait(plane_sem, len(column))

            @pl.when(has_left)
            def _():
                pl.semaphore_signal(next_sem, inc=1, **at(me, part - 1))

        if r == 1:

            @pl.when(has_right)
            def _():
                pl.semaphore_wait(next_sem, 1)

            onward(slot0_out, slot0_in, slot_sem.at[0])
            across(c0_out, c0_in, c_sem.at[0])

    def taken(ref, sem):
        some = ref.at[pl.ds(0, n_cont - 1)]
        pltpu.make_async_copy(some, some, sem).wait()

    def taken_here(ref, sem):
        @pl.when(has_left)
        def _():
            pltpu.make_async_copy(ref, ref, sem).wait()

    def by_bus(slot_sums):
        tall = jnp.concatenate(
            [slot_sums, jnp.zeros((16 - slot_sums.shape[0], slots), F32)], axis=0
        )
        wide = times(pieces(tall), listed[...])
        return [
            jnp.concatenate([wide[r : r + 1, j * LANES : (j + 1) * LANES] for j in range(blocks)], axis=0)
            for r in range(slot_sums.shape[0])
        ]

    loads_now = load[...]
    limits = limit[...]
    scale = 1.0 / (n_cont * conts)

    def update(x, mean_dual, beta, total):
        mean_gen = (x - mean_dual + balance * (loads_now + total * scale)) * inv_cost
        mean_dual = mean_dual + (mean_gen - x)
        beta = beta + (x + balance * loads_now - beta) * inv_cost - x
        return jnp.clip(mean_gen + mean_dual, 0.0, limits), mean_dual, beta

    taken(c0_in, c_sem.at[0, 1])
    taken_here(slot0_in, slot_sem.at[0, 1])
    total = jnp.sum(c0_in[...], axis=0)
    moved = by_bus(jnp.sum(slot0_in[...], axis=0))
    state = (base_v[...], total[2] * scale, jnp.zeros_like(loads_now))
    for r in range(2):
        state = update(*state, total[r] + moved[r])

    lefts = []
    for s in range(STREAMS):

        @pl.when(has_left)
        def _():
            right_copy(ROUNDS - 1, s).wait_recv()

        lefts.append(in_left[ROUNDS - 1, s])
    spread = times(pieces(jnp.concatenate(lefts, axis=0)), listed[...])
    theta_o[...] = now - spread * inv_degree
    net = net + spread
    part_gen = (balance * net - dual_part) * inv_row

    for r in range(2, ROUNDS):
        if r == ROUNDS - 1:
            x, _, beta = state
            row_gen = (x - beta + balance * loads_now) * inv_cost
            for j in range(blocks):
                cols = slice(j * LANES, (j + 1) * LANES)
                gen_o[:, cols] = part_gen[:, cols] + row_gen[j : j + 1, :]
        taken(c_in.at[r - 2], c_sem.at[r - 1, 1])
        taken_here(slot_in.at[r - 2], slot_sem.at[r - 1, 1])
        total = jnp.sum(c_in[r - 2], axis=0)
        moved = by_bus(jnp.sum(slot_in[r - 2], axis=0))
        state = update(*state, total + moved[0])
    base_o[...] = state[0]

    @pl.when(has_left)
    def _():
        for s in range(STREAMS):
            pick(s).wait_send()
            for r in range(ROUNDS - 1):
                left_copy(r, s).wait_send()
        count_l.wait_send()

    @pl.when(has_right)
    def _():
        for s in range(STREAMS):
            for r in range(ROUNDS):
                right_copy(r, s).wait_send()
        count_r.wait_send()
        pltpu.make_async_copy(slot0_in, slot0_in, slot_sem.at[0, 0]).wait()
        for r in range(2, ROUNDS):
            pltpu.make_async_copy(slot_in.at[r - 2], slot_in.at[r - 2], slot_sem.at[r - 1, 0]).wait()

    taken(c0_in, c_sem.at[0, 0])
    for r in range(2, ROUNDS):
        taken(c_in.at[r - 2], c_sem.at[r - 1, 0])


def finish(theta, gen, base, theta_o, gen_o, base_o, sem):
    copies = [pltpu.make_async_copy(base, base_o, sem.at[0])]
    rows = theta.shape[0] // CHUNKS
    for i in range(CHUNKS):
        part = pl.ds(i * rows, rows)
        copies.append(pltpu.make_async_copy(theta.at[part], theta_o.at[part], sem.at[1 + i]))
        copies.append(pltpu.make_async_copy(gen.at[part], gen_o.at[part], sem.at[1 + CHUNKS + i]))
    for copy in copies:
        copy.start()
    for copy in copies:
        copy.wait()


def local(
    n_cont,
    n_net,
    angles,
    lam_from,
    lam_to,
    gen_dual,
    base_prev,
    outage,
    from_bus,
    to_ref,
    halo_rows,
    stiffness,
    bus_load,
    gen_cost,
    gen_limit,
):
    conts, buses = angles.shape
    branches = from_bus.shape[0]
    slots = halo_rows.shape[0]
    blocks = buses // LANES
    row = n_cont
    for r in range(1, n_cont + 1):
        if n_cont % r == 0 and r * r <= n_cont:
            row = r

    def by_lanes(v):
        return v.reshape(v.shape[0] // LANES, LANES)

    inside = pl.BlockSpec(memory_space=pltpu.VMEM)
    outside = pl.BlockSpec(memory_space=pltpu.HBM)
    dma = pltpu.SemaphoreType.DMA
    vmem = pltpu.VMEM
    i32 = jnp.int32
    kept = pl.pallas_call(
        functools.partial(kernel, n_cont, n_net, row),
        out_shape=(
            pltpu.VMEM((conts, buses), F32),
            pltpu.VMEM((conts, buses), F32),
            pltpu.VMEM((blocks, LANES), F32),
        ),
        in_specs=[outside] * 13,
        out_specs=(inside,) * 3,
        scratch_shapes=[
            vmem((conts, buses), F32),
            vmem((conts, branches), F32),
            vmem((conts, branches), F32),
            vmem((conts, buses), F32),
            vmem((conts, branches), i32),
            vmem((branches // LANES, LANES), i32),
            vmem((branches // LANES, LANES), i32),
            vmem((1, slots), i32),
            vmem((branches // LANES, LANES), F32),
            vmem((blocks, LANES), F32),
            vmem((blocks, LANES), F32),
            vmem((blocks, LANES), F32),
            vmem((blocks, LANES), F32),
            vmem((buses, branches), BF16),
            vmem((buses, branches), BF16),
            vmem((2 * slots, branches), BF16),
            vmem((2 * slots, branches), BF16),
            vmem((slots, buses), BF16),
            vmem((STREAMS, conts // STREAMS, slots), F32),
            vmem((STREAMS, conts // STREAMS, slots), F32),
            vmem((2, 8, slots), F32),
            vmem((2, 8, slots), F32),
            vmem((ROUNDS, STREAMS, conts // STREAMS, slots), F32),
            vmem((ROUNDS, STREAMS, conts // STREAMS, slots), F32),
            vmem((ROUNDS, STREAMS, conts // STREAMS, slots), F32),
            vmem((ROUNDS, STREAMS, conts // STREAMS, slots), F32),
            vmem((3, blocks, LANES), F32),
            vmem((n_cont, 3, blocks, LANES), F32),
            vmem((2, blocks, LANES), F32),
            vmem((2, n_cont, blocks, LANES), F32),
            vmem((2, slots), F32),
            vmem((n_cont, 2, slots), F32),
            vmem((2, 1, slots), F32),
            vmem((2, n_cont, 1, slots), F32),
            dma((13,)),
            dma((2, STREAMS)),
            dma((2,)),
            dma((2,)),
            dma((ROUNDS, STREAMS)),
            dma((ROUNDS, STREAMS)),
            dma((ROUNDS, STREAMS)),
            dma((ROUNDS, STREAMS)),
            dma((3, 2)),
            dma((3, 2)),
            pltpu.SemaphoreType.REGULAR,
            pltpu.SemaphoreType.REGULAR,
        ],
        compiler_params=pltpu.CompilerParams(
            collective_id=0, has_side_effects=True
        ),
        name="rounds",
    )(
        angles,
        lam_from,
        lam_to,
        gen_dual,
        outage,
        by_lanes(from_bus),
        by_lanes(to_ref),
        by_lanes(halo_rows),
        by_lanes(stiffness),
        by_lanes(base_prev),
        by_lanes(bus_load),
        by_lanes(gen_cost),
        by_lanes(gen_limit),
    )
    theta, generation, base = pl.pallas_call(
        finish,
        out_shape=(
            jax.ShapeDtypeStruct((conts, buses), F32),
            jax.ShapeDtypeStruct((conts, buses), F32),
            jax.ShapeDtypeStruct((blocks, LANES), F32),
        ),
        in_specs=[inside] * 3,
        out_specs=(outside,) * 3,
        scratch_shapes=[dma((1 + 2 * CHUNKS,))],
        compiler_params=pltpu.CompilerParams(vmem_limit_bytes=4 << 20),
        name="finish",
    )(*kept)
    return theta, generation, base.reshape(buses)


def solution(mesh):
    both = P("cont", "net")
    one = P("net")
    placed = (both, both, both, both, one, both, one, one, one, one, one, one, one)
    return jax.shard_map(
        functools.partial(local, mesh.shape["cont"], mesh.shape["net"]),
        mesh=mesh,
        in_specs=placed,
        out_specs=(both, both, one),
        check_vma=False,
    )
```

```python
import functools

import jax
import jax.numpy as jnp
from jax import lax
from jax.experimental import pallas as pl
from jax.experimental.pallas import tpu as pltpu
from jax.sharding import PartitionSpec as P

ROUNDS = 4
LANES = 128
STREAMS = 2
CHUNKS = 1
penalty = 1.0
balance = 2.0
F32 = jnp.float32
BF16 = jnp.bfloat16
MESH = pl.DeviceIdType.MESH


def pieces(x):
    high = x.astype(BF16)
    low = (x - high.astype(F32)).astype(BF16)
    return jnp.concatenate([high, low], axis=0)


def fold(y):
    half = y.shape[0] // 2
    return y[:half] + y[half:]


def times(x2, table):
    return fold(jnp.dot(x2, table, preferred_element_type=F32))


def times_t(x2, table):
    return fold(
        lax.dot_general(x2, table, (((1,), (1,)), ((), ())), preferred_element_type=F32)
    )


def is_at(a, b):
    return jnp.where(a == b, 1.0, 0.0).astype(F32)


def kernel(
    n_cont,
    n_net,
    row,
    angles_h,
    lam_f_h,
    lam_t_h,
    dual_h,
    outage_h,
    from_h,
    to_h,
    rows_h,
    stiff_h,
    base_h,
    load_h,
    cost_h,
    limit_h,
    theta_o,
    gen_o,
    base_o,
    theta,
    lam_f,
    lam_t,
    dual,
    outage,
    from_v,
    to_v,
    rows_v,
    stiff,
    base_v,
    load,
    cost,
    limit,
    own,
    count,
    edge,
    edge_count,
    listed,
    pick_out,
    pick_in,
    count_out,
    count_in,
    out_left,
    out_right,
    in_left,
    in_right,
    c0_out,
    c0_in,
    c_out,
    c_in,
    slot0_out,
    slot0_in,
    slot_out,
    slot_in,
    zeros,
    where_at,
    if_any,
    in_sem,
    pick_sem,
    count_send,
    count_recv,
    send_l,
    recv_l,
    send_r,
    recv_r,
    c_sem,
    slot_sem,
    plane_sem,
    next_sem,
):
    conts, buses = theta.shape
    branches = lam_f.shape[1]
    slots = rows_v.shape[1]
    blocks = buses // LANES
    part_rows = conts // STREAMS
    me = lax.axis_index("cont")
    part = lax.axis_index("net")
    has_left = part > 0
    has_right = part < n_net - 1
    my_row, my_col = lax.div(me, row), lax.rem(me, row)
    n_rows = n_cont // row

    def at(c, p):
        return dict(device_id={"cont": c, "net": p}, device_id_type=MESH)

    loads = []
    for i, (src, dst) in enumerate(
        [
            (rows_h, rows_v),
            (angles_h, theta),
            (from_h, from_v),
            (to_h, to_v),
            (lam_f_h, lam_f),
            (lam_t_h, lam_t),
            (outage_h, outage),
            (stiff_h, stiff),
            (dual_h, dual),
            (base_h, base_v),
            (load_h, load),
            (cost_h, cost),
            (limit_h, limit),
        ]
    ):
        copy = pltpu.make_async_copy(src, dst, in_sem.at[i])
        copy.start()
        loads.append(copy)

    barrier = pltpu.get_barrier_semaphore()
    column = [lax.rem(my_row + j, n_rows) * row + my_col for j in range(1, n_rows)]
    near = [my_row * row + lax.rem(my_col + j, row) for j in range(1, row)] + column

    @pl.when(has_left)
    def _():
        pl.semaphore_signal(barrier, inc=1, **at(me, part - 1))

    @pl.when(has_right)
    def _():
        pl.semaphore_signal(barrier, inc=1, **at(me, part + 1))

    for c in near:
        pl.semaphore_signal(barrier, inc=1, **at(c, part))

    def hops(step):
        return min(step[0], n_rows - step[0]) + min(step[1], row - step[1])

    steps = sorted(((i, j) for i in range(n_rows) for j in range(row)), key=hops, reverse=True)
    plane = [
        lax.rem(my_row + i, n_rows) * row + lax.rem(my_col + j, row) for i, j in steps
    ]

    loads[0].wait()
    rows = rows_v[...]
    rows = jnp.where(rows < buses, rows, -1)
    bus_id = lax.broadcasted_iota(jnp.int32, (buses, slots), 0)
    listed[...] = is_at(bus_id, rows).astype(BF16)
    loads[1].wait()
    theta0 = theta[...]
    theta2 = pieces(theta0)
    picked = times(theta2, listed[...])
    for s in range(STREAMS):
        pick_out[s] = picked[s * part_rows : (s + 1) * part_rows]

    inner = has_left & has_right

    @pl.when(inner)
    def _():
        pl.semaphore_wait(barrier, len(near) + 2)

    @pl.when(jnp.logical_not(inner))
    def _():
        pl.semaphore_wait(barrier, len(near) + 1)

    def to_left(src, dst, s, r):
        return pltpu.make_async_remote_copy(src, dst, s, r, **at(me, part - 1))

    def to_right(src, dst, s, r):
        return pltpu.make_async_remote_copy(src, dst, s, r, **at(me, part + 1))

    def pick(s):
        return to_left(pick_out.at[s], pick_in.at[s], pick_sem.at[0, s], pick_sem.at[1, s])

    def left_copy(r, s):
        return to_left(out_left.at[r, s], in_right.at[r, s], send_l.at[r, s], recv_l.at[r, s])

    def right_copy(r, s):
        return to_right(out_right.at[r, s], in_left.at[r, s], send_r.at[r, s], recv_r.at[r, s])

    @pl.when(has_left)
    def _():
        for s in range(STREAMS):
            pick(s).start()

    def nothing(dst, sem):
        pltpu.make_async_copy(zeros.at[pl.ds(0, dst.shape[0])], dst, sem).start()

    zeros[...] = jnp.zeros_like(zeros)

    @pl.when(jnp.logical_not(has_left))
    def _():
        slot0_in[...] = jnp.zeros_like(slot0_in)
        slot_in[...] = jnp.zeros_like(slot_in)
        nothing(count_in.at[0], count_recv.at[1])
        for r in range(ROUNDS):
            for s in range(STREAMS):
                nothing(in_left.at[r, s], recv_r.at[r, s])

    @pl.when(jnp.logical_not(has_right))
    def _():
        nothing(count_in.at[1], count_recv.at[0])
        for s in range(STREAMS):
            nothing(pick_in.at[s], pick_sem.at[1, s])
            for r in range(ROUNDS - 1):
                nothing(in_right.at[r, s], recv_l.at[r, s])

    for c in column:
        pl.semaphore_signal(plane_sem, inc=1, **at(c, part))

    rows_c = jnp.transpose(jnp.broadcast_to(rows.astype(F32), (slots, slots))).astype(jnp.int32)
    slot_id = lax.broadcasted_iota(jnp.int32, (slots, LANES), 0)
    loads[2].wait()
    loads[3].wait()
    for j in range(branches // LANES):
        cols = slice(j * LANES, (j + 1) * LANES)
        start = from_v[j : j + 1, :]
        end = to_v[j : j + 1, :]
        a, b = is_at(rows_c, start), is_at(rows_c, end)
        edge[:slots, cols] = (a - b).astype(BF16)
        edge_count[:slots, cols] = (a + b).astype(BF16)
        c = is_at(slot_id + buses, end)
        edge[slots:, cols] = (-c).astype(BF16)
        edge_count[slots:, cols] = c.astype(BF16)

    ones = jnp.ones((16, branches), BF16)
    counts = lax.dot_general(
        ones, edge_count[...], (((1,), (1,)), ((), ())), preferred_element_type=F32
    )
    listed_count, slot_count = counts[:8, :slots], counts[:8, slots:]
    count_out[0] = listed_count
    count_out[1] = slot_count
    count_l = to_left(count_out.at[0], count_in.at[1], count_send.at[0], count_recv.at[0])
    count_r = to_right(count_out.at[1], count_in.at[0], count_send.at[1], count_recv.at[1])

    @pl.when(has_left)
    def _():
        count_l.start()

    @pl.when(has_right)
    def _():
        count_r.start()

    kind = lax.broadcasted_iota(jnp.int32, (16, slots), 0)
    probe = jnp.where(kind == 0, lax.broadcasted_iota(jnp.int32, (16, slots), 1), kind)
    probe = jnp.where(kind < 2, probe, 0).astype(F32).astype(BF16)
    differ = jnp.dot(probe, edge[:slots, :], preferred_element_type=F32)
    both = jnp.dot(probe, edge_count[:slots, :], preferred_element_type=F32)
    ends = [0.5 * (both + differ), 0.5 * (both - differ)]
    for j in range(branches // LANES):
        cols = slice(j * LANES, (j + 1) * LANES)
        for k in range(2):
            where_at[k, j] = jnp.broadcast_to(ends[k][0:1, cols], (8, LANES)).astype(jnp.int32)
            if_any[k, j] = jnp.broadcast_to(ends[k][1:2, cols], (8, LANES))
        beyond = jnp.broadcast_to(to_v[j : j + 1, :] - buses, (8, LANES))
        where_at[2, j] = jnp.maximum(beyond, 0)
        if_any[2, j] = jnp.where(beyond >= 0, 1.0, 0.0).astype(F32)

    def reach(values, k, j):
        times_8 = part_rows // 8
        index = jnp.concatenate([where_at[k, j]] * times_8, axis=0)
        mask = jnp.concatenate([if_any[k, j]] * times_8, axis=0)
        return mask * jnp.take_along_axis(values, index, axis=1)

    def reached(values, change=None):
        out = []
        for j in range(branches // LANES):
            gap = -reach(values, 2, j)
            if change is not None:
                gap = gap + (reach(change, 0, j) - reach(change, 1, j))
            out.append(gap)
        return jnp.concatenate(out, axis=1)

    for j in range(branches // LANES):
        cols = slice(j * LANES, (j + 1) * LANES)
        a = is_at(bus_id, from_v[j : j + 1, :])
        b = is_at(bus_id, to_v[j : j + 1, :])
        own[:, cols] = (a - b).astype(BF16)
        count[:, cols] = (a + b).astype(BF16)
    delta = times(theta2, own[...])

    for copy in loads[4:]:
        copy.wait()
    share = []
    for j in range(branches // LANES):
        cols = slice(j * LANES, (j + 1) * LANES)
        full = stiff[j : j + 1, :]
        full = full / (penalty + 2.0 * full)
        share.append(full * (1.0 - outage[:, cols].astype(F32)))
    share = jnp.concatenate(share, axis=1)
    rest = delta - (lam_f[...] - lam_t[...])

    own_count = lax.dot_general(
        ones, count[...], (((1,), (1,)), ((), ())), preferred_element_type=F32
    )[:1]
    inv_cost = 1.0 / (cost[...] + (penalty + balance))
    dual_part = dual[...]
    inv_row = jnp.concatenate([inv_cost[j : j + 1, :] for j in range(blocks)], axis=1)

    def store_sums(dst, values):
        sums = jnp.sum(values, axis=0, keepdims=True)
        for j in range(blocks):
            dst[j : j + 1, :] = sums[:, j * LANES : (j + 1) * LANES]

    store_sums(c0_out.at[2], dual_part)

    def across(src, dst, sem):
        dst[me] = src[...]
        for c in plane[:-1]:
            pltpu.make_async_remote_copy(
                src, dst.at[me], sem.at[0], sem.at[1], **at(c, part)
            ).start()

    def onward(src, dst, sem):
        @pl.when(has_right)
        def _():
            for c in plane:
                pltpu.make_async_remote_copy(
                    src, dst.at[me], sem.at[0], sem.at[1], **at(c, part + 1)
                ).start()

    halos = [None] * STREAMS
    slot_nets = [None] * STREAMS
    now = theta0
    net = None
    for r in range(ROUNDS):
        last = r == ROUNDS - 1
        lefts, flows, deltas = [], [], []
        for s in range(STREAMS):
            block = slice(s * part_rows, (s + 1) * part_rows)

            if r == 0:
                pick(s).wait_recv()
            else:
                left_copy(r - 1, s).wait_recv()
                right_copy(r - 1, s).wait_recv()
            if r == 0:
                halos[s] = pick_in[s]
                added = reached(halos[s])
                deltas.append(delta[block] + added)
                flows.append(share[block] * (rest[block] + added))
            else:
                left = in_left[r - 1, s]
                lefts.append(left)
                halos[s] = keep_halo * halos[s] - (in_right[r - 1, s] + slot_nets[s]) * inv_halo
                gap = rest[block] + 2.0 * reached(halos[s], -left * inv_listed)
                deltas.append(0.5 * (gap + delta[block]) - flow[block])
                flows.append(share[block] * gap)
            if last:
                continue
            sent = times_t(pieces(flows[s]), edge[...])
            slot_nets[s] = sent[:, slots:]
            out_right[r, s] = slot_nets[s]
            out_left[r, s] = sent[:, :slots]

            @pl.when(has_right)
            def _():
                right_copy(r, s).start()

            @pl.when(has_left)
            def _():
                left_copy(r, s).start()

        flow = jnp.concatenate(flows, axis=0)
        delta = jnp.concatenate(deltas, axis=0)
        flow2 = pieces(flow)
        if last:
            slot_net = times_t(flow2, edge[slots:, :])
        else:
            slot_net = jnp.concatenate(slot_nets, axis=0)
        slot_sum = jnp.sum(slot_net, axis=0, keepdims=True)
        if r < 2:
            slot0_out[r : r + 1, :] = slot_sum
        else:
            slot_out[r - 2] = slot_sum
            onward(slot_out.at[r - 2], slot_in.at[r - 2], slot_sem.at[r - 1])
        if last:
            for s in range(STREAMS):
                out_right[r, s] = slot_net[s * part_rows : (s + 1) * part_rows]

            @pl.when(has_right)
            def _():
                for s in range(STREAMS):
                    right_copy(r, s).start()

        net_here = times_t(flow2, own[...])
        store_sums(c0_out.at[r] if r < 2 else c_out.at[r - 2], net_here)
        if r >= 2:
            across(c_out.at[r - 2], c_in.at[r - 2], c_sem.at[r - 1])

        if r == 0:

            count_l.wait_recv()
            count_r.wait_recv()
            left_count = count_in[0]
            inv_halo = 1.0 / (count_in[1][:1] + slot_count[:1] + 1.0)
            keep_halo = 1.0 - inv_halo
            inv_listed = 1.0 / (listed_count[:1] + left_count[:1] + 1.0)
            left_count = jnp.concatenate([left_count, left_count], axis=0)
            degree = own_count + times_t(pieces(left_count), listed[...])[:1]
            inv_degree = 1.0 / (degree + 1.0)
            keep = 1.0 - inv_degree
        else:
            spread = times_t(pieces(jnp.concatenate(lefts, axis=0)), listed[...])
            net = net + spread
            now = now - spread * inv_degree
            dual_part = dual_part - (dual_part - 2.0 * net) * inv_row

        net = net_here
        now = keep * now - net * inv_degree
        if not last:
            rest = 2.0 * times(pieces(now), own[...]) + (2.0 * flow - delta)
        if r == 0:
            pl.semaphore_wait(plane_sem, len(column))

            @pl.when(has_left)
            def _():
                pl.semaphore_signal(next_sem, inc=1, **at(me, part - 1))

        if r == 1:

            @pl.when(has_right)
            def _():
                pl.semaphore_wait(next_sem, 1)

            onward(slot0_out, slot0_in, slot_sem.at[0])
            across(c0_out, c0_in, c_sem.at[0])

    def taken(ref, sem):
        some = ref.at[pl.ds(0, n_cont - 1)]
        pltpu.make_async_copy(some, some, sem).wait()

    def taken_here(ref, sem):
        @pl.when(has_left)
        def _():
            pltpu.make_async_copy(ref, ref, sem).wait()

    def by_bus(slot_sums):
        tall = jnp.concatenate(
            [slot_sums, jnp.zeros((16 - slot_sums.shape[0], slots), F32)], axis=0
        )
        wide = times_t(pieces(tall), listed[...])
        return [
            jnp.concatenate([wide[r : r + 1, j * LANES : (j + 1) * LANES] for j in range(blocks)], axis=0)
            for r in range(slot_sums.shape[0])
        ]

    loads_now = load[...]
    limits = limit[...]
    scale = 1.0 / (n_cont * conts)

    def update(x, mean_dual, beta, total):
        mean_gen = (x - mean_dual + balance * (loads_now + total * scale)) * inv_cost
        mean_dual = mean_dual + (mean_gen - x)
        beta = beta + (x + balance * loads_now - beta) * inv_cost - x
        return jnp.clip(mean_gen + mean_dual, 0.0, limits), mean_dual, beta

    taken(c0_in, c_sem.at[0, 1])
    taken_here(slot0_in, slot_sem.at[0, 1])
    total = jnp.sum(c0_in[...], axis=0)
    moved = by_bus(jnp.sum(slot0_in[...], axis=0))
    state = (base_v[...], total[2] * scale, jnp.zeros_like(loads_now))
    for r in range(2):
        state = update(*state, total[r] + moved[r])

    lefts = []
    for s in range(STREAMS):
        right_copy(ROUNDS - 1, s).wait_recv()
        lefts.append(in_left[ROUNDS - 1, s])
    spread = times_t(pieces(jnp.concatenate(lefts, axis=0)), listed[...])
    theta_o[...] = now - spread * inv_degree
    net = net + spread
    part_gen = (balance * net - dual_part) * inv_row

    for r in range(2, ROUNDS):
        if r == ROUNDS - 1:
            x, _, beta = state
            row_gen = (x - beta + balance * loads_now) * inv_cost
            for j in range(blocks):
                cols = slice(j * LANES, (j + 1) * LANES)
                gen_o[:, cols] = part_gen[:, cols] + row_gen[j : j + 1, :]
        taken(c_in.at[r - 2], c_sem.at[r - 1, 1])
        taken_here(slot_in.at[r - 2], slot_sem.at[r - 1, 1])
        total = jnp.sum(c_in[r - 2], axis=0)
        moved = by_bus(jnp.sum(slot_in[r - 2], axis=0))
        state = update(*state, total + moved[0])
    base_o[...] = state[0]

    @pl.when(has_left)
    def _():
        for s in range(STREAMS):
            pick(s).wait_send()
            for r in range(ROUNDS - 1):
                left_copy(r, s).wait_send()
        count_l.wait_send()

    @pl.when(has_right)
    def _():
        for s in range(STREAMS):
            for r in range(ROUNDS):
                right_copy(r, s).wait_send()
        count_r.wait_send()
        pltpu.make_async_copy(slot0_in, slot0_in, slot_sem.at[0, 0]).wait()
        for r in range(2, ROUNDS):
            pltpu.make_async_copy(slot_in.at[r - 2], slot_in.at[r - 2], slot_sem.at[r - 1, 0]).wait()

    taken(c0_in, c_sem.at[0, 0])
    for r in range(2, ROUNDS):
        taken(c_in.at[r - 2], c_sem.at[r - 1, 0])


def finish(theta, gen, base, theta_o, gen_o, base_o, sem):
    copies = [pltpu.make_async_copy(base, base_o, sem.at[0])]
    rows = theta.shape[0] // CHUNKS
    for i in range(CHUNKS):
        part = pl.ds(i * rows, rows)
        copies.append(pltpu.make_async_copy(theta.at[part], theta_o.at[part], sem.at[1 + i]))
        copies.append(pltpu.make_async_copy(gen.at[part], gen_o.at[part], sem.at[1 + CHUNKS + i]))
    for copy in copies:
        copy.start()
    for copy in copies:
        copy.wait()


def local(
    n_cont,
    n_net,
    angles,
    lam_from,
    lam_to,
    gen_dual,
    base_prev,
    outage,
    from_bus,
    to_ref,
    halo_rows,
    stiffness,
    bus_load,
    gen_cost,
    gen_limit,
):
    conts, buses = angles.shape
    branches = from_bus.shape[0]
    slots = halo_rows.shape[0]
    blocks = buses // LANES
    row = n_cont
    for r in range(1, n_cont + 1):
        if n_cont % r == 0 and r * r <= n_cont:
            row = r

    def by_lanes(v):
        return v.reshape(v.shape[0] // LANES, LANES)

    inside = pl.BlockSpec(memory_space=pltpu.VMEM)
    outside = pl.BlockSpec(memory_space=pltpu.HBM)
    dma = pltpu.SemaphoreType.DMA
    vmem = pltpu.VMEM
    i32 = jnp.int32
    kept = pl.pallas_call(
        functools.partial(kernel, n_cont, n_net, row),
        out_shape=(
            pltpu.VMEM((conts, buses), F32),
            pltpu.VMEM((conts, buses), F32),
            pltpu.VMEM((blocks, LANES), F32),
        ),
        in_specs=[outside] * 13,
        out_specs=(inside,) * 3,
        scratch_shapes=[
            vmem((conts, buses), F32),
            vmem((conts, branches), F32),
            vmem((conts, branches), F32),
            vmem((conts, buses), F32),
            vmem((conts, branches), i32),
            vmem((branches // LANES, LANES), i32),
            vmem((branches // LANES, LANES), i32),
            vmem((1, slots), i32),
            vmem((branches // LANES, LANES), F32),
            vmem((blocks, LANES), F32),
            vmem((blocks, LANES), F32),
            vmem((blocks, LANES), F32),
            vmem((blocks, LANES), F32),
            vmem((buses, branches), BF16),
            vmem((buses, branches), BF16),
            vmem((2 * slots, branches), BF16),
            vmem((2 * slots, branches), BF16),
            vmem((buses, slots), BF16),
            vmem((STREAMS, conts // STREAMS, slots), F32),
            vmem((STREAMS, conts // STREAMS, slots), F32),
            vmem((2, 8, slots), F32),
            vmem((2, 8, slots), F32),
            vmem((ROUNDS, STREAMS, conts // STREAMS, slots), F32),
            vmem((ROUNDS, STREAMS, conts // STREAMS, slots), F32),
            vmem((ROUNDS, STREAMS, conts // STREAMS, slots), F32),
            vmem((ROUNDS, STREAMS, conts // STREAMS, slots), F32),
            vmem((3, blocks, LANES), F32),
            vmem((n_cont, 3, blocks, LANES), F32),
            vmem((2, blocks, LANES), F32),
            vmem((2, n_cont, blocks, LANES), F32),
            vmem((2, slots), F32),
            vmem((n_cont, 2, slots), F32),
            vmem((2, 1, slots), F32),
            vmem((2, n_cont, 1, slots), F32),
            vmem((conts, slots), F32),
            vmem((3, branches // LANES, 8, LANES), i32),
            vmem((3, branches // LANES, 8, LANES), F32),
            dma((13,)),
            dma((2, STREAMS)),
            dma((2,)),
            dma((2,)),
            dma((ROUNDS, STREAMS)),
            dma((ROUNDS, STREAMS)),
            dma((ROUNDS, STREAMS)),
            dma((ROUNDS, STREAMS)),
            dma((3, 2)),
            dma((3, 2)),
            pltpu.SemaphoreType.REGULAR,
            pltpu.SemaphoreType.REGULAR,
        ],
        compiler_params=pltpu.CompilerParams(
            collective_id=0, has_side_effects=True
        ),
        name="rounds",
    )(
        angles,
        lam_from,
        lam_to,
        gen_dual,
        outage,
        by_lanes(from_bus),
        by_lanes(to_ref),
        by_lanes(halo_rows),
        by_lanes(stiffness),
        by_lanes(base_prev),
        by_lanes(bus_load),
        by_lanes(gen_cost),
        by_lanes(gen_limit),
    )
    theta, generation, base = pl.pallas_call(
        finish,
        out_shape=(
            jax.ShapeDtypeStruct((conts, buses), F32),
            jax.ShapeDtypeStruct((conts, buses), F32),
            jax.ShapeDtypeStruct((blocks, LANES), F32),
        ),
        in_specs=[inside] * 3,
        out_specs=(outside,) * 3,
        scratch_shapes=[dma((1 + 2 * CHUNKS,))],
        compiler_params=pltpu.CompilerParams(vmem_limit_bytes=4 << 20),
        name="finish",
    )(*kept)
    return theta, generation, base.reshape(buses)


def solution(mesh):
    both = P("cont", "net")
    one = P("net")
    placed = (both, both, both, both, one, both, one, one, one, one, one, one, one)
    return jax.shard_map(
        functools.partial(local, mesh.shape["cont"], mesh.shape["net"]),
        mesh=mesh,
        in_specs=placed,
        out_specs=(both, both, one),
        check_vma=False,
    )
```

```python
import functools

import jax
import jax.numpy as jnp
from jax import lax
from jax.experimental import pallas as pl
from jax.experimental.pallas import tpu as pltpu
from jax.sharding import PartitionSpec as P

ROUNDS = 4
LANES = 128
STREAMS = 2
CHUNKS = 1
penalty = 1.0
balance = 2.0
F32 = jnp.float32
BF16 = jnp.bfloat16
MESH = pl.DeviceIdType.MESH


def pieces(x):
    high = x.astype(BF16)
    low = (x - high.astype(F32)).astype(BF16)
    return jnp.concatenate([high, low], axis=0)


def fold(y):
    half = y.shape[0] // 2
    return y[:half] + y[half:]


def times(x2, table):
    return fold(jnp.dot(x2, table, preferred_element_type=F32))


def times_t(x2, table):
    return fold(
        lax.dot_general(x2, table, (((1,), (1,)), ((), ())), preferred_element_type=F32)
    )


def is_at(a, b):
    return jnp.where(a == b, 1.0, 0.0).astype(F32)


def kernel(
    n_cont,
    n_net,
    row,
    angles_h,
    lam_f_h,
    lam_t_h,
    dual_h,
    outage_h,
    from_h,
    to_h,
    rows_h,
    stiff_h,
    base_h,
    load_h,
    cost_h,
    limit_h,
    theta_o,
    gen_o,
    base_o,
    theta,
    lam,
    dual,
    outage,
    ends_v,
    rows_v,
    stiff,
    params,
    own,
    count,
    edge,
    edge_count,
    listed,
    pick_out,
    pick_in,
    count_out,
    count_in,
    out_left,
    out_right,
    inbox,
    last_out,
    last_in,
    c0_out,
    c0_in,
    c_out,
    c_in,
    slot0_out,
    slot0_in,
    slot_out,
    slot_in,
    zeros,
    where_at,
    if_any,
    sem,
    pick_sem,
    count_sem,
    in_sem,
    last_sem,
    c_sem,
    slot_sem,
    plane_sem,
    next_sem,
):
    conts, buses = theta.shape
    branches = outage.shape[1]
    slots = rows_v.shape[1]
    blocks = buses // LANES
    part_rows = conts // STREAMS
    me = lax.axis_index("cont")
    part = lax.axis_index("net")
    has_left = part > 0
    has_right = part < n_net - 1
    my_row, my_col = lax.div(me, row), lax.rem(me, row)
    n_rows = n_cont // row

    def at(c, p):
        return dict(device_id={"cont": c, "net": p}, device_id_type=MESH)

    for src, dst, i in [
        (rows_h, rows_v, 0),
        (angles_h, theta, 1),
        (from_h, ends_v.at[0], 2),
        (to_h, ends_v.at[1], 2),
        (lam_f_h, lam.at[0], 3),
        (lam_t_h, lam.at[1], 3),
        (outage_h, outage, 4),
        (stiff_h, stiff, 5),
        (dual_h, dual, 6),
        (base_h, params.at[0], 7),
        (load_h, params.at[1], 7),
        (cost_h, params.at[2], 7),
        (limit_h, params.at[3], 7),
    ]:
        pltpu.make_async_copy(src, dst, sem.at[i]).start()

    def loaded(ref, i):
        pltpu.make_async_copy(ref, ref, sem.at[i]).wait()

    barrier = pltpu.get_barrier_semaphore()
    column = [lax.rem(my_row + j, n_rows) * row + my_col for j in range(1, n_rows)]
    near = [my_row * row + lax.rem(my_col + j, row) for j in range(1, row)] + column

    @pl.when(has_left)
    def _():
        pl.semaphore_signal(barrier, inc=1, **at(me, part - 1))

    @pl.when(has_right)
    def _():
        pl.semaphore_signal(barrier, inc=1, **at(me, part + 1))

    for c in near:
        pl.semaphore_signal(barrier, inc=1, **at(c, part))

    def hops(step):
        return min(step[0], n_rows - step[0]) + min(step[1], row - step[1])

    steps = sorted(((i, j) for i in range(n_rows) for j in range(row)), key=hops, reverse=True)
    plane = [
        lax.rem(my_row + i, n_rows) * row + lax.rem(my_col + j, row) for i, j in steps
    ]

    loaded(rows_v, 0)
    rows = rows_v[...]
    rows = jnp.where(rows < buses, rows, -1)
    bus_id = lax.broadcasted_iota(jnp.int32, (buses, slots), 0)
    listed[...] = is_at(bus_id, rows).astype(BF16)
    loaded(theta, 1)
    theta0 = theta[...]
    theta2 = pieces(theta0)
    picked = times(theta2, listed[...])
    for s in range(STREAMS):
        pick_out[s] = picked[s * part_rows : (s + 1) * part_rows]

    inner = has_left & has_right

    @pl.when(inner)
    def _():
        pl.semaphore_wait(barrier, len(near) + 2)

    @pl.when(jnp.logical_not(inner))
    def _():
        pl.semaphore_wait(barrier, len(near) + 1)

    def to_left(src, dst, s, r):
        return pltpu.make_async_remote_copy(src, dst, s, r, **at(me, part - 1))

    def to_right(src, dst, s, r):
        return pltpu.make_async_remote_copy(src, dst, s, r, **at(me, part + 1))

    def pick(s):
        return to_left(pick_out.at[s], pick_in.at[s], sem.at[s], pick_sem.at[s])

    def left_copy(r, s):
        return to_left(out_left.at[r, s], inbox.at[r, s, 1], sem.at[3 + s], in_sem.at[r, s])

    def right_copy(r, s):
        return to_right(out_right.at[r, s], inbox.at[r, s, 0], sem.at[3 + STREAMS + s], in_sem.at[r, s])

    last_copy = to_right(last_out, last_in, sem.at[3], last_sem)
    local_send = sem.at[3 + 2 * STREAMS]
    slot_send = sem.at[4 + 2 * STREAMS]

    @pl.when(has_left)
    def _():
        for s in range(STREAMS):
            pick(s).start()

    def nothing(dst, sem):
        pltpu.make_async_copy(zeros.at[pl.ds(0, dst.shape[0])], dst, sem).start()

    zeros[...] = jnp.zeros_like(zeros)

    @pl.when(jnp.logical_not(has_left))
    def _():
        slot0_in[...] = jnp.zeros_like(slot0_in)
        slot_in[...] = jnp.zeros_like(slot_in)
        nothing(count_in.at[0], count_sem)
        nothing(last_in, last_sem)
        for r in range(ROUNDS - 1):
            for s in range(STREAMS):
                nothing(inbox.at[r, s, 0], in_sem.at[r, s])

    @pl.when(jnp.logical_not(has_right))
    def _():
        nothing(count_in.at[1], count_sem)
        for s in range(STREAMS):
            nothing(pick_in.at[s], pick_sem.at[s])
            for r in range(ROUNDS - 1):
                nothing(inbox.at[r, s, 1], in_sem.at[r, s])

    for c in column:
        pl.semaphore_signal(plane_sem, inc=1, **at(c, part))

    rows_c = jnp.transpose(jnp.broadcast_to(rows.astype(F32), (slots, slots))).astype(jnp.int32)
    slot_id = lax.broadcasted_iota(jnp.int32, (slots, LANES), 0)
    loaded(ends_v, 2)
    from_v, to_v = ends_v.at[0], ends_v.at[1]
    for j in range(branches // LANES):
        cols = slice(j * LANES, (j + 1) * LANES)
        start = from_v[j : j + 1, :]
        end = to_v[j : j + 1, :]
        a, b = is_at(rows_c, start), is_at(rows_c, end)
        edge[:slots, cols] = (a - b).astype(BF16)
        edge_count[:slots, cols] = (a + b).astype(BF16)
        c = is_at(slot_id + buses, end)
        edge[slots:, cols] = (-c).astype(BF16)
        edge_count[slots:, cols] = c.astype(BF16)

    ones = jnp.ones((16, branches), BF16)
    counts = lax.dot_general(
        ones, edge_count[...], (((1,), (1,)), ((), ())), preferred_element_type=F32
    )
    listed_count, slot_count = counts[:8, :slots], counts[:8, slots:]
    count_out[0] = listed_count
    count_out[1] = slot_count
    count_l = to_left(count_out.at[0], count_in.at[1], sem.at[2], count_sem)
    count_r = to_right(count_out.at[1], count_in.at[0], slot_send, count_sem)

    @pl.when(has_left)
    def _():
        count_l.start()

    @pl.when(has_right)
    def _():
        count_r.start()

    kind = lax.broadcasted_iota(jnp.int32, (16, slots), 0)
    probe = jnp.where(kind == 0, lax.broadcasted_iota(jnp.int32, (16, slots), 1), kind)
    probe = jnp.where(kind < 2, probe, 0).astype(F32).astype(BF16)
    differ = jnp.dot(probe, edge[:slots, :], preferred_element_type=F32)
    both = jnp.dot(probe, edge_count[:slots, :], preferred_element_type=F32)
    ends = [0.5 * (both + differ), 0.5 * (both - differ)]
    of_bus = lax.dot_general(
        probe, listed[...], (((1,), (1,)), ((), ())), preferred_element_type=F32
    )
    fill = [jnp.zeros((8 - blocks, LANES), F32)]

    def in_blocks(v):
        return jnp.concatenate([v[:, j * LANES : (j + 1) * LANES] for j in range(blocks)] + fill, axis=0)

    bus_slot = in_blocks(of_bus[0:1]).astype(jnp.int32)
    bus_listed = in_blocks(of_bus[1:2])
    for j in range(branches // LANES):
        cols = slice(j * LANES, (j + 1) * LANES)
        for k in range(2):
            where_at[k, j] = jnp.broadcast_to(ends[k][0:1, cols], (8, LANES)).astype(jnp.int32)
            if_any[k, j] = jnp.broadcast_to(ends[k][1:2, cols], (8, LANES))
        beyond = jnp.broadcast_to(to_v[j : j + 1, :] - buses, (8, LANES))
        where_at[2, j] = jnp.maximum(beyond, 0)
        if_any[2, j] = jnp.where(beyond >= 0, 1.0, 0.0).astype(F32)

    def reach(values, k, j):
        times_8 = part_rows // 8
        index = jnp.concatenate([where_at[k, j]] * times_8, axis=0)
        mask = jnp.concatenate([if_any[k, j]] * times_8, axis=0)
        return mask * jnp.take_along_axis(values, index, axis=1)

    def reached(values, change=None):
        out = []
        for j in range(branches // LANES):
            gap = -reach(values, 2, j)
            if change is not None:
                gap = gap + (reach(change, 0, j) - reach(change, 1, j))
            out.append(gap)
        return jnp.concatenate(out, axis=1)

    for j in range(branches // LANES):
        cols = slice(j * LANES, (j + 1) * LANES)
        a = is_at(bus_id, from_v[j : j + 1, :])
        b = is_at(bus_id, to_v[j : j + 1, :])
        own[:, cols] = (a - b).astype(BF16)
    delta = times(theta2, own[...])

    for ref, i in [(lam, 3), (outage, 4), (stiff, 5), (dual, 6), (params, 7)]:
        loaded(ref, i)
    share = []
    for j in range(branches // LANES):
        cols = slice(j * LANES, (j + 1) * LANES)
        full = stiff[j : j + 1, :]
        full = full / (penalty + 2.0 * full)
        share.append(full * (1.0 - outage[:, cols].astype(F32)))
    share = jnp.concatenate(share, axis=1)
    rest = delta - (lam[0] - lam[1])

    inv_cost = 1.0 / (params[2] + (penalty + balance))
    dual_part = dual[...]
    inv_row = jnp.concatenate([inv_cost[j : j + 1, :] for j in range(blocks)], axis=1)

    def store_sums(dst, values):
        sums = jnp.sum(values, axis=0, keepdims=True)
        for j in range(blocks):
            dst[j : j + 1, :] = sums[:, j * LANES : (j + 1) * LANES]

    store_sums(c0_out.at[2], dual_part)

    def across(src, dst, arrived):
        dst[me] = src[...]
        for c in plane[:-1]:
            pltpu.make_async_remote_copy(
                src, dst.at[me], local_send, arrived, **at(c, part)
            ).start()

    def onward(src, dst, arrived):
        @pl.when(has_right)
        def _():
            for c in plane:
                pltpu.make_async_remote_copy(
                    src, dst.at[me], slot_send, arrived, **at(c, part + 1)
                ).start()

    def taken(ref, arrived):
        some = ref.at[pl.ds(0, n_cont - 1)]
        pltpu.make_async_copy(some, some, arrived).wait()

    def onward_sent(ref):
        @pl.when(has_right)
        def _():
            pltpu.make_async_copy(ref, ref, slot_send).wait()

    halos = [None] * STREAMS
    slot_nets = [None] * STREAMS
    now = theta0
    net = None
    for r in range(ROUNDS):
        last = r == ROUNDS - 1
        lefts, flows, deltas = [], [], []
        for s in range(STREAMS):
            block = slice(s * part_rows, (s + 1) * part_rows)

            if r == 0:
                pick(s).wait_recv()
            else:
                box = inbox.at[r - 1, s]
                pltpu.make_async_copy(box, box, in_sem.at[r - 1, s]).wait()
            if r == 0:
                halos[s] = pick_in[s]
                added = reached(halos[s])
                deltas.append(delta[block] + added)
                flows.append(share[block] * (rest[block] + added))
            else:
                left = inbox[r - 1, s, 0]
                lefts.append(left)
                halos[s] = keep_halo * halos[s] - (inbox[r - 1, s, 1] + slot_nets[s]) * inv_halo
                gap = rest[block] + 2.0 * reached(halos[s], -left * inv_listed)
                deltas.append(0.5 * (gap + delta[block]) - flow[block])
                flows.append(share[block] * gap)
            if last:
                continue
            sent = times_t(pieces(flows[s]), edge[...])
            slot_nets[s] = sent[:, slots:]
            out_right[r, s] = slot_nets[s]
            out_left[r, s] = sent[:, :slots]

            @pl.when(has_right)
            def _():
                right_copy(r, s).start()

            @pl.when(has_left)
            def _():
                left_copy(r, s).start()

        flow = jnp.concatenate(flows, axis=0)
        delta = jnp.concatenate(deltas, axis=0)
        flow2 = pieces(flow)
        if last:
            whole = jnp.broadcast_to(jnp.sum(flow, axis=0, keepdims=True), (16, branches))
            whole2 = pieces(whole)
            slot_sum = times_t(whole2, edge[slots:, :])[:1]
        else:
            slot_net = jnp.concatenate(slot_nets, axis=0)
            slot_sum = jnp.sum(slot_net, axis=0, keepdims=True)
        if r < 2:
            slot0_out[r : r + 1, :] = slot_sum
        else:
            slot_out[r - 2] = slot_sum
            if not last:
                onward_sent(slot0_in)
            onward(slot_out.at[r - 2], slot_in.at[r - 2], slot_sem.at[r - 1])
        if last:
            store_sums(c_out.at[1], times_t(whole2, own[...])[:1])
            across(c_out.at[1], c_in.at[1], c_sem.at[2])
            slot_net = times_t(flow2, edge[slots:, :])
            last_out[...] = slot_net

            @pl.when(has_right)
            def _():
                last_copy.start()

        net_here = times_t(flow2, own[...])
        if r < 2:
            store_sums(c0_out.at[r], net_here)
        elif not last:
            store_sums(c_out.at[0], net_here)
            taken(c0_in, local_send)
            across(c_out.at[0], c_in.at[0], c_sem.at[1])

        if r == 0:

            for j in range(branches // LANES):
                cols = slice(j * LANES, (j + 1) * LANES)
                a = is_at(bus_id, from_v[j : j + 1, :])
                b = is_at(bus_id, to_v[j : j + 1, :])
                count[:, cols] = (a + b).astype(BF16)
            own_count = lax.dot_general(
                ones, count[...], (((1,), (1,)), ((), ())), preferred_element_type=F32
            )[:1]
            pltpu.make_async_copy(count_in, count_in, count_sem).wait()

            @pl.when(has_left)
            def _():
                for s in range(STREAMS):
                    pick(s).wait_send()
                count_l.wait_send()

            @pl.when(has_right)
            def _():
                count_r.wait_send()

            left_count = count_in[0]
            inv_halo = 1.0 / (count_in[1][:1] + slot_count[:1] + 1.0)
            keep_halo = 1.0 - inv_halo
            inv_listed = 1.0 / (listed_count[:1] + left_count[:1] + 1.0)
            left_count = jnp.concatenate([left_count, left_count], axis=0)
            degree = own_count + times_t(pieces(left_count), listed[...])[:1]
            inv_degree = 1.0 / (degree + 1.0)
            keep = 1.0 - inv_degree
        else:
            spread = times_t(pieces(jnp.concatenate(lefts, axis=0)), listed[...])
            net = net + spread
            now = now - spread * inv_degree
            dual_part = dual_part - (dual_part - 2.0 * net) * inv_row

        net = net_here
        now = keep * now - net * inv_degree
        if not last:
            rest = 2.0 * times(pieces(now), own[...]) + (2.0 * flow - delta)
        if not last:

            @pl.when(has_left)
            def _():
                for s in range(STREAMS):
                    left_copy(r, s).wait_send()

            @pl.when(has_right)
            def _():
                for s in range(STREAMS):
                    right_copy(r, s).wait_send()

        if r == 2:
            taken(c_in.at[0], local_send)
            onward_sent(slot_in.at[0])
        if r == 0:
            pl.semaphore_wait(plane_sem, len(column))

            @pl.when(has_left)
            def _():
                pl.semaphore_signal(next_sem, inc=1, **at(me, part - 1))

        if r == 1:

            @pl.when(has_right)
            def _():
                pl.semaphore_wait(next_sem, 1)

            onward(slot0_out, slot0_in, slot_sem.at[0])
            across(c0_out, c0_in, c_sem.at[0])

    def taken_here(ref, arrived):
        @pl.when(has_left)
        def _():
            pltpu.make_async_copy(ref, ref, arrived).wait()

    def by_bus(slot_sums):
        tall = jnp.broadcast_to(slot_sums, (8, slots))
        return (bus_listed * jnp.take_along_axis(tall, bus_slot, axis=1))[:blocks]

    loads_now = params[1]
    limits = params[3]
    scale = 1.0 / (n_cont * conts)

    def update(x, mean_dual, beta, total):
        mean_gen = (x - mean_dual + balance * (loads_now + total * scale)) * inv_cost
        mean_dual = mean_dual + (mean_gen - x)
        beta = beta + (x + balance * loads_now - beta) * inv_cost - x
        return jnp.clip(mean_gen + mean_dual, 0.0, limits), mean_dual, beta

    taken(c0_in, c_sem.at[0])
    taken_here(slot0_in, slot_sem.at[0])
    total = jnp.sum(c0_in[...], axis=0)
    moved = jnp.sum(slot0_in[...], axis=0)
    state = (params[0], total[2] * scale, jnp.zeros_like(loads_now))
    for r in range(2):
        state = update(*state, total[r] + by_bus(moved[r : r + 1]))

    last_copy.wait_recv()
    spread = times_t(pieces(last_in[...]), listed[...])
    theta_o[...] = now - spread * inv_degree
    net = net + spread
    part_gen = (balance * net - dual_part) * inv_row

    @pl.when(has_right)
    def _():
        last_copy.wait_send()

    for r in range(2, ROUNDS):
        if r == ROUNDS - 1:
            x, _, beta = state
            row_gen = (x - beta + balance * loads_now) * inv_cost
            for j in range(blocks):
                cols = slice(j * LANES, (j + 1) * LANES)
                gen_o[:, cols] = part_gen[:, cols] + row_gen[j : j + 1, :]
        taken(c_in.at[r - 2], c_sem.at[r - 1])
        taken_here(slot_in.at[r - 2], slot_sem.at[r - 1])
        total = jnp.sum(c_in[r - 2], axis=0)
        state = update(*state, total + by_bus(jnp.sum(slot_in[r - 2], axis=0)))
    base_o[...] = state[0]

    onward_sent(slot_in.at[1])
    taken(c_in.at[1], local_send)


def finish(theta, gen, base, theta_o, gen_o, base_o, sem):
    copies = [pltpu.make_async_copy(base, base_o, sem.at[0])]
    rows = theta.shape[0] // CHUNKS
    for i in range(CHUNKS):
        part = pl.ds(i * rows, rows)
        copies.append(pltpu.make_async_copy(theta.at[part], theta_o.at[part], sem.at[1 + i]))
        copies.append(pltpu.make_async_copy(gen.at[part], gen_o.at[part], sem.at[1 + CHUNKS + i]))
    for copy in copies:
        copy.start()
    for copy in copies:
        copy.wait()


def local(
    n_cont,
    n_net,
    angles,
    lam_from,
    lam_to,
    gen_dual,
    base_prev,
    outage,
    from_bus,
    to_ref,
    halo_rows,
    stiffness,
    bus_load,
    gen_cost,
    gen_limit,
):
    conts, buses = angles.shape
    branches = from_bus.shape[0]
    slots = halo_rows.shape[0]
    blocks = buses // LANES
    row = n_cont
    for r in range(1, n_cont + 1):
        if n_cont % r == 0 and r * r <= n_cont:
            row = r

    def by_lanes(v):
        return v.reshape(v.shape[0] // LANES, LANES)

    inside = pl.BlockSpec(memory_space=pltpu.VMEM)
    outside = pl.BlockSpec(memory_space=pltpu.HBM)
    dma = pltpu.SemaphoreType.DMA
    vmem = pltpu.VMEM
    i32 = jnp.int32
    kept = pl.pallas_call(
        functools.partial(kernel, n_cont, n_net, row),
        out_shape=(
            pltpu.VMEM((conts, buses), F32),
            pltpu.VMEM((conts, buses), F32),
            pltpu.VMEM((blocks, LANES), F32),
        ),
        in_specs=[outside] * 13,
        out_specs=(inside,) * 3,
        scratch_shapes=[
            vmem((conts, buses), F32),
            vmem((2, conts, branches), F32),
            vmem((conts, buses), F32),
            vmem((conts, branches), i32),
            vmem((2, branches // LANES, LANES), i32),
            vmem((1, slots), i32),
            vmem((branches // LANES, LANES), F32),
            vmem((4, blocks, LANES), F32),
            vmem((buses, branches), BF16),
            vmem((buses, branches), BF16),
            vmem((2 * slots, branches), BF16),
            vmem((2 * slots, branches), BF16),
            vmem((buses, slots), BF16),
            vmem((STREAMS, conts // STREAMS, slots), F32),
            vmem((STREAMS, conts // STREAMS, slots), F32),
            vmem((2, 8, slots), F32),
            vmem((2, 8, slots), F32),
            vmem((ROUNDS - 1, STREAMS, conts // STREAMS, slots), F32),
            vmem((ROUNDS - 1, STREAMS, conts // STREAMS, slots), F32),
            vmem((ROUNDS - 1, STREAMS, 2, conts // STREAMS, slots), F32),
            vmem((conts, slots), F32),
            vmem((conts, slots), F32),
            vmem((3, blocks, LANES), F32),
            vmem((n_cont, 3, blocks, LANES), F32),
            vmem((2, blocks, LANES), F32),
            vmem((2, n_cont, blocks, LANES), F32),
            vmem((2, slots), F32),
            vmem((n_cont, 2, slots), F32),
            vmem((2, 1, slots), F32),
            vmem((2, n_cont, 1, slots), F32),
            vmem((conts, slots), F32),
            vmem((3, branches // LANES, 8, LANES), i32),
            vmem((3, branches // LANES, 8, LANES), F32),
            dma((5 + 2 * STREAMS,)),
            dma((STREAMS,)),
            dma,
            dma((ROUNDS - 1, STREAMS)),
            dma,
            dma((3,)),
            dma((3,)),
            pltpu.SemaphoreType.REGULAR,
            pltpu.SemaphoreType.REGULAR,
        ],
        compiler_params=pltpu.CompilerParams(
            collective_id=0, has_side_effects=True
        ),
        name="rounds",
    )(
        angles,
        lam_from,
        lam_to,
        gen_dual,
        outage,
        by_lanes(from_bus),
        by_lanes(to_ref),
        by_lanes(halo_rows),
        by_lanes(stiffness),
        by_lanes(base_prev),
        by_lanes(bus_load),
        by_lanes(gen_cost),
        by_lanes(gen_limit),
    )
    theta, generation, base = pl.pallas_call(
        finish,
        out_shape=(
            jax.ShapeDtypeStruct((conts, buses), F32),
            jax.ShapeDtypeStruct((conts, buses), F32),
            jax.ShapeDtypeStruct((blocks, LANES), F32),
        ),
        in_specs=[inside] * 3,
        out_specs=(outside,) * 3,
        scratch_shapes=[dma((1 + 2 * CHUNKS,))],
        compiler_params=pltpu.CompilerParams(vmem_limit_bytes=4 << 20),
        name="finish",
    )(*kept)
    return theta, generation, base.reshape(buses)


def solution(mesh):
    both = P("cont", "net")
    one = P("net")
    placed = (both, both, both, both, one, both, one, one, one, one, one, one, one)
    return jax.shard_map(
        functools.partial(local, mesh.shape["cont"], mesh.shape["net"]),
        mesh=mesh,
        in_specs=placed,
        out_specs=(both, both, one),
        check_vma=False,
    )
```

```python
import functools

import jax
import jax.numpy as jnp
from jax import lax
from jax.experimental import pallas as pl
from jax.experimental.pallas import tpu as pltpu
from jax.sharding import PartitionSpec as P

ROUNDS = 4
LANES = 128
STREAMS = 2
CHUNKS = 1
penalty = 1.0
balance = 2.0
F32 = jnp.float32
BF16 = jnp.bfloat16
MESH = pl.DeviceIdType.MESH


def pieces(x):
    high = x.astype(BF16)
    low = (x - high.astype(F32)).astype(BF16)
    return jnp.concatenate([high, low], axis=0)


def fold(y):
    half = y.shape[0] // 2
    return y[:half] + y[half:]


def times(x2, table):
    return fold(jnp.dot(x2, table, preferred_element_type=F32))


def times_t(x2, table):
    return fold(
        lax.dot_general(x2, table, (((1,), (1,)), ((), ())), preferred_element_type=F32)
    )


def is_at(a, b):
    return jnp.where(a == b, 1.0, 0.0).astype(F32)


def kernel(
    n_cont,
    n_net,
    row,
    angles_h,
    lam_f_h,
    lam_t_h,
    dual_h,
    outage_h,
    from_h,
    to_h,
    rows_h,
    stiff_h,
    base_h,
    load_h,
    cost_h,
    limit_h,
    theta_o,
    gen_o,
    base_o,
    theta,
    lam,
    dual,
    outage,
    ends_v,
    rows_v,
    stiff,
    params,
    own,
    count,
    edge,
    edge_count,
    listed,
    pick_out,
    pick_in,
    count_out,
    count_in,
    out_left,
    out_right,
    inbox,
    last_out,
    last_in,
    c0_out,
    c0_in,
    c_out,
    c_in,
    slot0_out,
    slot0_in,
    slot_out,
    slot_in,
    zeros,
    where_at,
    if_any,
    sem,
    pick_sem,
    count_sem,
    in_sem,
    last_sem,
    c_sem,
    slot_sem,
    plane_sem,
    next_sem,
):
    conts, buses = theta.shape
    branches = outage.shape[1]
    slots = rows_v.shape[1]
    blocks = buses // LANES
    part_rows = conts // STREAMS
    me = lax.axis_index("cont")
    part = lax.axis_index("net")
    has_left = part > 0
    has_right = part < n_net - 1
    my_row, my_col = lax.div(me, row), lax.rem(me, row)
    n_rows = n_cont // row

    def at(c, p):
        return dict(device_id={"cont": c, "net": p}, device_id_type=MESH)

    for src, dst, i in [
        (rows_h, rows_v, 0),
        (angles_h, theta, 1),
        (from_h, ends_v.at[0], 2),
        (to_h, ends_v.at[1], 2),
        (lam_f_h, lam.at[0], 3),
        (lam_t_h, lam.at[1], 3),
        (outage_h, outage, 4),
        (stiff_h, stiff, 5),
        (dual_h, dual, 6),
        (base_h, params.at[0], 7),
        (load_h, params.at[1], 7),
        (cost_h, params.at[2], 7),
        (limit_h, params.at[3], 7),
    ]:
        pltpu.make_async_copy(src, dst, sem.at[i]).start()

    def loaded(ref, i):
        pltpu.make_async_copy(ref, ref, sem.at[i]).wait()

    barrier = pltpu.get_barrier_semaphore()
    column = [lax.rem(my_row + j, n_rows) * row + my_col for j in range(1, n_rows)]
    near = [my_row * row + lax.rem(my_col + j, row) for j in range(1, row)] + column

    @pl.when(has_left)
    def _():
        pl.semaphore_signal(barrier, inc=1, **at(me, part - 1))

    @pl.when(has_right)
    def _():
        pl.semaphore_signal(barrier, inc=1, **at(me, part + 1))

    for c in near:
        pl.semaphore_signal(barrier, inc=1, **at(c, part))

    def hops(step):
        return min(step[0], n_rows - step[0]) + min(step[1], row - step[1])

    steps = sorted(((i, j) for i in range(n_rows) for j in range(row)), key=hops, reverse=True)
    plane = [
        lax.rem(my_row + i, n_rows) * row + lax.rem(my_col + j, row) for i, j in steps
    ]

    loaded(rows_v, 0)
    rows = rows_v[...]
    rows = jnp.where(rows < buses, rows, -1)
    bus_id = lax.broadcasted_iota(jnp.int32, (buses, slots), 0)
    listed[...] = is_at(bus_id, rows).astype(BF16)
    loaded(theta, 1)
    theta0 = theta[...]
    theta2 = pieces(theta0)
    picked = times(theta2, listed[...])
    for s in range(STREAMS):
        pick_out[s] = picked[s * part_rows : (s + 1) * part_rows]

    inner = has_left & has_right

    @pl.when(inner)
    def _():
        pl.semaphore_wait(barrier, len(near) + 2)

    @pl.when(jnp.logical_not(inner))
    def _():
        pl.semaphore_wait(barrier, len(near) + 1)

    def to_left(src, dst, s, r):
        return pltpu.make_async_remote_copy(src, dst, s, r, **at(me, part - 1))

    def to_right(src, dst, s, r):
        return pltpu.make_async_remote_copy(src, dst, s, r, **at(me, part + 1))

    def pick(s):
        return to_left(pick_out.at[s], pick_in.at[s], sem.at[s], pick_sem.at[s])

    def left_copy(r, s):
        return to_left(out_left.at[r, s], inbox.at[r, s, 1], sem.at[3 + s], in_sem.at[r, s])

    def right_copy(r, s):
        return to_right(out_right.at[r, s], inbox.at[r, s, 0], sem.at[3 + STREAMS + s], in_sem.at[r, s])

    last_copy = to_right(last_out, last_in, sem.at[3], last_sem)
    local_send = sem.at[3 + 2 * STREAMS]
    slot_send = sem.at[4 + 2 * STREAMS]

    @pl.when(has_left)
    def _():
        for s in range(STREAMS):
            pick(s).start()

    def nothing(dst, sem):
        pltpu.make_async_copy(zeros.at[pl.ds(0, dst.shape[0])], dst, sem).start()

    zeros[...] = jnp.zeros_like(zeros)

    @pl.when(jnp.logical_not(has_left))
    def _():
        slot0_in[...] = jnp.zeros_like(slot0_in)
        slot_in[...] = jnp.zeros_like(slot_in)
        nothing(count_in.at[0], count_sem)
        nothing(last_in, last_sem)
        for r in range(ROUNDS - 1):
            for s in range(STREAMS):
                nothing(inbox.at[r, s, 0], in_sem.at[r, s])

    @pl.when(jnp.logical_not(has_right))
    def _():
        nothing(count_in.at[1], count_sem)
        for s in range(STREAMS):
            nothing(pick_in.at[s], pick_sem.at[s])
            for r in range(ROUNDS - 1):
                nothing(inbox.at[r, s, 1], in_sem.at[r, s])

    for c in column:
        pl.semaphore_signal(plane_sem, inc=1, **at(c, part))

    rows_c = jnp.transpose(jnp.broadcast_to(rows.astype(F32), (slots, slots))).astype(jnp.int32)
    slot_id = lax.broadcasted_iota(jnp.int32, (slots, LANES), 0)
    loaded(ends_v, 2)
    from_v, to_v = ends_v.at[0], ends_v.at[1]
    for j in range(branches // LANES):
        cols = slice(j * LANES, (j + 1) * LANES)
        start = from_v[j : j + 1, :]
        end = to_v[j : j + 1, :]
        a, b = is_at(rows_c, start), is_at(rows_c, end)
        edge[:slots, cols] = (a - b).astype(BF16)
        edge_count[:slots, cols] = (a + b).astype(BF16)
        c = is_at(slot_id + buses, end)
        edge[slots:, cols] = (-c).astype(BF16)
        edge_count[slots:, cols] = c.astype(BF16)

    ones = jnp.ones((16, branches), BF16)
    counts = lax.dot_general(
        ones, edge_count[...], (((1,), (1,)), ((), ())), preferred_element_type=F32
    )
    listed_count, slot_count = counts[:8, :slots], counts[:8, slots:]
    count_out[0] = listed_count
    count_out[1] = slot_count
    count_l = to_left(count_out.at[0], count_in.at[1], sem.at[2], count_sem)
    count_r = to_right(count_out.at[1], count_in.at[0], slot_send, count_sem)

    @pl.when(has_left)
    def _():
        count_l.start()

    @pl.when(has_right)
    def _():
        count_r.start()

    kind = lax.broadcasted_iota(jnp.int32, (16, slots), 0)
    probe = jnp.where(kind == 0, lax.broadcasted_iota(jnp.int32, (16, slots), 1), kind)
    probe = jnp.where(kind < 2, probe, 0).astype(F32).astype(BF16)
    differ = jnp.dot(probe, edge[:slots, :], preferred_element_type=F32)
    both = jnp.dot(probe, edge_count[:slots, :], preferred_element_type=F32)
    ends = [0.5 * (both + differ), 0.5 * (both - differ)]
    of_bus = lax.dot_general(
        probe, listed[...], (((1,), (1,)), ((), ())), preferred_element_type=F32
    )
    fill = [jnp.zeros((8 - blocks, LANES), F32)]

    def in_blocks(v):
        return jnp.concatenate([v[:, j * LANES : (j + 1) * LANES] for j in range(blocks)] + fill, axis=0)

    bus_slot = in_blocks(of_bus[0:1]).astype(jnp.int32)
    bus_listed = in_blocks(of_bus[1:2])
    for j in range(branches // LANES):
        cols = slice(j * LANES, (j + 1) * LANES)
        for k in range(2):
            where_at[k, j] = jnp.broadcast_to(ends[k][0:1, cols], (8, LANES)).astype(jnp.int32)
            if_any[k, j] = jnp.broadcast_to(ends[k][1:2, cols], (8, LANES))
        beyond = jnp.broadcast_to(to_v[j : j + 1, :] - buses, (8, LANES))
        where_at[2, j] = jnp.maximum(beyond, 0)
        if_any[2, j] = jnp.where(beyond >= 0, 1.0, 0.0).astype(F32)

    def reach(values, k, j):
        times_8 = part_rows // 8
        index = jnp.concatenate([where_at[k, j]] * times_8, axis=0)
        mask = jnp.concatenate([if_any[k, j]] * times_8, axis=0)
        return mask * jnp.take_along_axis(values, index, axis=1)

    def reached(values, change=None):
        out = []
        for j in range(branches // LANES):
            gap = -reach(values, 2, j)
            if change is not None:
                gap = gap + (reach(change, 0, j) - reach(change, 1, j))
            out.append(gap)
        return jnp.concatenate(out, axis=1)

    for j in range(branches // LANES):
        cols = slice(j * LANES, (j + 1) * LANES)
        a = is_at(bus_id, from_v[j : j + 1, :])
        b = is_at(bus_id, to_v[j : j + 1, :])
        own[:, cols] = (a - b).astype(BF16)
    delta = times(theta2, own[...])

    for ref, i in [(lam, 3), (outage, 4), (stiff, 5), (dual, 6), (params, 7)]:
        loaded(ref, i)
    share = []
    for j in range(branches // LANES):
        cols = slice(j * LANES, (j + 1) * LANES)
        full = stiff[j : j + 1, :]
        full = full / (penalty + 2.0 * full)
        share.append(full * (1.0 - outage[:, cols].astype(F32)))
    share = jnp.concatenate(share, axis=1)
    rest = delta - (lam[0] - lam[1])

    inv_cost = 1.0 / (params[2] + (penalty + balance))
    dual_part = dual[...]
    inv_row = jnp.concatenate([inv_cost[j : j + 1, :] for j in range(blocks)], axis=1)

    def store_sums(dst, values):
        sums = jnp.sum(values, axis=0, keepdims=True)
        for j in range(blocks):
            dst[j : j + 1, :] = sums[:, j * LANES : (j + 1) * LANES]

    store_sums(c0_out.at[2], dual_part)

    def across(src, dst, arrived):
        dst[me] = src[...]
        for c in plane[:-1]:
            pltpu.make_async_remote_copy(
                src, dst.at[me], local_send, arrived, **at(c, part)
            ).start()

    def onward(src, dst, arrived):
        @pl.when(has_right)
        def _():
            for c in plane:
                pltpu.make_async_remote_copy(
                    src, dst.at[me], slot_send, arrived, **at(c, part + 1)
                ).start()

    def taken(ref, arrived):
        some = ref.at[pl.ds(0, n_cont - 1)]
        pltpu.make_async_copy(some, some, arrived).wait()

    def onward_sent(ref):
        @pl.when(has_right)
        def _():
            pltpu.make_async_copy(ref, ref, slot_send).wait()

    halos = [None] * STREAMS
    slot_nets = [None] * STREAMS
    now = theta0
    net = None
    for r in range(ROUNDS):
        last = r == ROUNDS - 1
        lefts, flows, deltas = [], [], []
        for s in range(STREAMS):
            block = slice(s * part_rows, (s + 1) * part_rows)

            if r == 0:
                pick(s).wait_recv()
            else:
                box = inbox.at[r - 1, s]
                pltpu.make_async_copy(box, box, in_sem.at[r - 1, s]).wait()
            if r == 0:
                halos[s] = pick_in[s]
                added = reached(halos[s])
                deltas.append(delta[block] + added)
                flows.append(share[block] * (rest[block] + added))
            else:
                left = inbox[r - 1, s, 0]
                lefts.append(left)
                halos[s] = keep_halo * halos[s] - (inbox[r - 1, s, 1] + slot_nets[s]) * inv_halo
                gap = rest[block] + 2.0 * reached(halos[s], -left * inv_listed)
                deltas.append(0.5 * (gap + delta[block]) - flow[block])
                flows.append(share[block] * gap)
            if last:
                continue
            sent = times_t(pieces(flows[s]), edge[...])
            slot_nets[s] = sent[:, slots:]
            out_right[r, s] = slot_nets[s]
            out_left[r, s] = sent[:, :slots]

            @pl.when(has_right)
            def _():
                right_copy(r, s).start()

            @pl.when(has_left)
            def _():
                left_copy(r, s).start()

        flow = jnp.concatenate(flows, axis=0)
        delta = jnp.concatenate(deltas, axis=0)
        flow2 = pieces(flow)
        if last:
            whole = jnp.broadcast_to(jnp.sum(flow, axis=0, keepdims=True), (16, branches))
            whole2 = pieces(whole)
            slot_sum = times_t(whole2, edge[slots:, :])[:1]
        else:
            slot_net = jnp.concatenate(slot_nets, axis=0)
            slot_sum = jnp.sum(slot_net, axis=0, keepdims=True)
        if last:
            store_sums(c_out.at[1], times_t(whole2, own[...])[:1])
            across(c_out.at[1], c_in.at[1], c_sem.at[2])
        if r < 2:
            slot0_out[r : r + 1, :] = slot_sum
        else:
            slot_out[r - 2] = slot_sum
            if not last:
                onward_sent(slot0_in)
            onward(slot_out.at[r - 2], slot_in.at[r - 2], slot_sem.at[r - 1])
        if last:
            slot_net = times_t(flow2, edge[slots:, :])
            last_out[...] = slot_net

            @pl.when(has_right)
            def _():
                last_copy.start()

        net_here = times_t(flow2, own[...])
        if r < 2:
            store_sums(c0_out.at[r], net_here)
        elif not last:
            store_sums(c_out.at[0], net_here)
            taken(c0_in, local_send)
            across(c_out.at[0], c_in.at[0], c_sem.at[1])

        if r == 0:

            for j in range(branches // LANES):
                cols = slice(j * LANES, (j + 1) * LANES)
                a = is_at(bus_id, from_v[j : j + 1, :])
                b = is_at(bus_id, to_v[j : j + 1, :])
                count[:, cols] = (a + b).astype(BF16)
            own_count = lax.dot_general(
                ones, count[...], (((1,), (1,)), ((), ())), preferred_element_type=F32
            )[:1]
            pltpu.make_async_copy(count_in, count_in, count_sem).wait()

            @pl.when(has_left)
            def _():
                for s in range(STREAMS):
                    pick(s).wait_send()
                count_l.wait_send()

            @pl.when(has_right)
            def _():
                count_r.wait_send()

            left_count = count_in[0]
            inv_halo = 1.0 / (count_in[1][:1] + slot_count[:1] + 1.0)
            keep_halo = 1.0 - inv_halo
            inv_listed = 1.0 / (listed_count[:1] + left_count[:1] + 1.0)
            left_count = jnp.concatenate([left_count, left_count], axis=0)
            degree = own_count + times_t(pieces(left_count), listed[...])[:1]
            inv_degree = 1.0 / (degree + 1.0)
            keep = 1.0 - inv_degree
        else:
            spread = times_t(pieces(jnp.concatenate(lefts, axis=0)), listed[...])
            net = net + spread
            now = now - spread * inv_degree
            dual_part = dual_part - (dual_part - 2.0 * net) * inv_row

        net = net_here
        now = keep * now - net * inv_degree
        if not last:
            rest = 2.0 * times(pieces(now), own[...]) + (2.0 * flow - delta)
        if not last:

            @pl.when(has_left)
            def _():
                for s in range(STREAMS):
                    left_copy(r, s).wait_send()

            @pl.when(has_right)
            def _():
                for s in range(STREAMS):
                    right_copy(r, s).wait_send()

        if r == 2:
            taken(c_in.at[0], local_send)
            onward_sent(slot_in.at[0])
        if r == 0:
            pl.semaphore_wait(plane_sem, len(column))

            @pl.when(has_left)
            def _():
                pl.semaphore_signal(next_sem, inc=1, **at(me, part - 1))

        if r == 1:

            @pl.when(has_right)
            def _():
                pl.semaphore_wait(next_sem, 1)

            onward(slot0_out, slot0_in, slot_sem.at[0])
            across(c0_out, c0_in, c_sem.at[0])

    def taken_here(ref, arrived):
        @pl.when(has_left)
        def _():
            pltpu.make_async_copy(ref, ref, arrived).wait()

    def by_bus(slot_sums):
        tall = jnp.broadcast_to(slot_sums, (8, slots))
        return (bus_listed * jnp.take_along_axis(tall, bus_slot, axis=1))[:blocks]

    loads_now = params[1]
    limits = params[3]
    scale = 1.0 / (n_cont * conts)

    def update(x, mean_dual, beta, total):
        mean_gen = (x - mean_dual + balance * (loads_now + total * scale)) * inv_cost
        mean_dual = mean_dual + (mean_gen - x)
        beta = beta + (x + balance * loads_now - beta) * inv_cost - x
        return jnp.clip(mean_gen + mean_dual, 0.0, limits), mean_dual, beta

    taken(c0_in, c_sem.at[0])
    taken_here(slot0_in, slot_sem.at[0])
    total = jnp.sum(c0_in[...], axis=0)
    moved = jnp.sum(slot0_in[...], axis=0)
    state = (params[0], total[2] * scale, jnp.zeros_like(loads_now))
    for r in range(2):
        state = update(*state, total[r] + by_bus(moved[r : r + 1]))

    last_copy.wait_recv()
    spread = times_t(pieces(last_in[...]), listed[...])
    theta_o[...] = now - spread * inv_degree
    net = net + spread
    part_gen = (balance * net - dual_part) * inv_row

    @pl.when(has_right)
    def _():
        last_copy.wait_send()

    for r in range(2, ROUNDS):
        if r == ROUNDS - 1:
            x, _, beta = state
            row_gen = (x - beta + balance * loads_now) * inv_cost
            for j in range(blocks):
                cols = slice(j * LANES, (j + 1) * LANES)
                gen_o[:, cols] = part_gen[:, cols] + row_gen[j : j + 1, :]
        taken(c_in.at[r - 2], c_sem.at[r - 1])
        taken_here(slot_in.at[r - 2], slot_sem.at[r - 1])
        total = jnp.sum(c_in[r - 2], axis=0)
        state = update(*state, total + by_bus(jnp.sum(slot_in[r - 2], axis=0)))
    base_o[...] = state[0]

    onward_sent(slot_in.at[1])
    taken(c_in.at[1], local_send)


def finish(theta, gen, base, theta_o, gen_o, base_o, sem):
    copies = [pltpu.make_async_copy(base, base_o, sem.at[0])]
    rows = theta.shape[0] // CHUNKS
    for i in range(CHUNKS):
        part = pl.ds(i * rows, rows)
        copies.append(pltpu.make_async_copy(theta.at[part], theta_o.at[part], sem.at[1 + i]))
        copies.append(pltpu.make_async_copy(gen.at[part], gen_o.at[part], sem.at[1 + CHUNKS + i]))
    for copy in copies:
        copy.start()
    for copy in copies:
        copy.wait()


def local(
    n_cont,
    n_net,
    angles,
    lam_from,
    lam_to,
    gen_dual,
    base_prev,
    outage,
    from_bus,
    to_ref,
    halo_rows,
    stiffness,
    bus_load,
    gen_cost,
    gen_limit,
):
    conts, buses = angles.shape
    branches = from_bus.shape[0]
    slots = halo_rows.shape[0]
    blocks = buses // LANES
    row = n_cont
    for r in range(1, n_cont + 1):
        if n_cont % r == 0 and r * r <= n_cont:
            row = r

    def by_lanes(v):
        return v.reshape(v.shape[0] // LANES, LANES)

    inside = pl.BlockSpec(memory_space=pltpu.VMEM)
    outside = pl.BlockSpec(memory_space=pltpu.HBM)
    dma = pltpu.SemaphoreType.DMA
    vmem = pltpu.VMEM
    i32 = jnp.int32
    kept = pl.pallas_call(
        functools.partial(kernel, n_cont, n_net, row),
        out_shape=(
            pltpu.VMEM((conts, buses), F32),
            pltpu.VMEM((conts, buses), F32),
            pltpu.VMEM((blocks, LANES), F32),
        ),
        in_specs=[outside] * 13,
        out_specs=(inside,) * 3,
        scratch_shapes=[
            vmem((conts, buses), F32),
            vmem((2, conts, branches), F32),
            vmem((conts, buses), F32),
            vmem((conts, branches), i32),
            vmem((2, branches // LANES, LANES), i32),
            vmem((1, slots), i32),
            vmem((branches // LANES, LANES), F32),
            vmem((4, blocks, LANES), F32),
            vmem((buses, branches), BF16),
            vmem((buses, branches), BF16),
            vmem((2 * slots, branches), BF16),
            vmem((2 * slots, branches), BF16),
            vmem((buses, slots), BF16),
            vmem((STREAMS, conts // STREAMS, slots), F32),
            vmem((STREAMS, conts // STREAMS, slots), F32),
            vmem((2, 8, slots), F32),
            vmem((2, 8, slots), F32),
            vmem((ROUNDS - 1, STREAMS, conts // STREAMS, slots), F32),
            vmem((ROUNDS - 1, STREAMS, conts // STREAMS, slots), F32),
            vmem((ROUNDS - 1, STREAMS, 2, conts // STREAMS, slots), F32),
            vmem((conts, slots), F32),
            vmem((conts, slots), F32),
            vmem((3, blocks, LANES), F32),
            vmem((n_cont, 3, blocks, LANES), F32),
            vmem((2, blocks, LANES), F32),
            vmem((2, n_cont, blocks, LANES), F32),
            vmem((2, slots), F32),
            vmem((n_cont, 2, slots), F32),
            vmem((2, 1, slots), F32),
            vmem((2, n_cont, 1, slots), F32),
            vmem((conts, slots), F32),
            vmem((3, branches // LANES, 8, LANES), i32),
            vmem((3, branches // LANES, 8, LANES), F32),
            dma((5 + 2 * STREAMS,)),
            dma((STREAMS,)),
            dma,
            dma((ROUNDS - 1, STREAMS)),
            dma,
            dma((3,)),
            dma((3,)),
            pltpu.SemaphoreType.REGULAR,
            pltpu.SemaphoreType.REGULAR,
        ],
        compiler_params=pltpu.CompilerParams(
            collective_id=0, has_side_effects=True
        ),
        name="rounds",
    )(
        angles,
        lam_from,
        lam_to,
        gen_dual,
        outage,
        by_lanes(from_bus),
        by_lanes(to_ref),
        by_lanes(halo_rows),
        by_lanes(stiffness),
        by_lanes(base_prev),
        by_lanes(bus_load),
        by_lanes(gen_cost),
        by_lanes(gen_limit),
    )
    theta, generation, base = pl.pallas_call(
        finish,
        out_shape=(
            jax.ShapeDtypeStruct((conts, buses), F32),
            jax.ShapeDtypeStruct((conts, buses), F32),
            jax.ShapeDtypeStruct((blocks, LANES), F32),
        ),
        in_specs=[inside] * 3,
        out_specs=(outside,) * 3,
        scratch_shapes=[dma((1 + 2 * CHUNKS,))],
        compiler_params=pltpu.CompilerParams(vmem_limit_bytes=4 << 20),
        name="finish",
    )(*kept)
    return theta, generation, base.reshape(buses)


def solution(mesh):
    both = P("cont", "net")
    one = P("net")
    placed = (both, both, both, both, one, both, one, one, one, one, one, one, one)
    return jax.shard_map(
        functools.partial(local, mesh.shape["cont"], mesh.shape["net"]),
        mesh=mesh,
        in_specs=placed,
        out_specs=(both, both, one),
        check_vma=False,
    )
```
